256 devices in a mesh: region: 2 (over core), cells: 128 (over z, y, x).
Axes of the slice: x: 4, y: 4, z: 8, core: 2. Of those that a mesh axis runs over, the one named last changes fastest.
Arguments:
- moments: float32 [2, 6, 4, 128, 16384], P('region', None, None, None, 'cells'), may hold values from 0 to 40, as said below
- courant_azimuth: float32 [2, 4, 128, 16384], P('region', None, None, 'cells'), may hold values from 0.1 to 0.3
- courant_radial: float32 [2, 4, 128, 16384], P('region', None, None, 'cells'), may hold values from -0.25 to 0.25
- courant_axial: float32 [2, 4, 128, 16384], P('region', None, None, 'cells'), may hold values from -0.2 to 0.2
- shear: float32 [2, 4, 128, 16384], P('region', None, None, 'cells'), may hold values from 0.5 to 4
- owner: int32 [2, 16384, 1], P('region', 'cells'), may hold values from 0 to 127; in each aligned block of 128 rows (0 to 127, 128 to 255, ..., all dimensions but the last counted through in order) at most 2 rows name the same one
- target: int32 [2, 16384], P('region', 'cells'), may hold values from 0 to 127
- ami_weight: float32 [2, 16384, 128, 128], P('region', 'cells'), may hold values from 0 to 1, as said below
Outputs:
- updated: float32 [2, 6, 4, 128, 16384], P('region', None, None, None, 'cells')
The draws below stay inside these ranges and needn't reach their ends.
Inputs may be any that keep to these rules, and one draw needn't show every extreme that they name: The rows of one device name each owner at most 2 times. Each cell's six entries are the moments of orders 0 to 5 of a positive measure on three or more sizes between 0.3 and 1.6. `ami_weight`: all entries are nonnegative.
All inputs are finite; a program needn't handle non-finite values.
Results may differ from the reference program's by a relative error of at most 0.0003.
Values sent between devices are 32-bit elements; how exact they have to be, the bound alone decides.
A program may use at most 64 MiB of HBM per device.

```python
import math
import jax
import jax.numpy as jnp
import numpy as np
from jax import lax

LAYERS = 4
ROWS = 128
FACES = 128
CAP = 2
AZIMUTH = 16384
BLOCKS = 16384
N_CELLS = 128


def draw_moments(key, part):
    shape = (2, LAYERS, ROWS, AZIMUTH)
    subkeys = jax.random.split(jax.random.fold_in(key, 11), 6)
    lower = (0.3, 0.7, 1.1)
    upper = (0.6, 1.0, 1.5)
    weight_lo = 0.01
    weight_hi = 1.2
    nodes = jnp.stack([jax.random.uniform(subkeys[index], shape, jnp.float32, lower[index], upper[index]) for index in range(3)])
    logs = jnp.stack([jax.random.uniform(subkeys[3 + index], shape, jnp.float32, jnp.log(weight_lo), jnp.log(weight_hi)) for index in range(3)])
    weights = jnp.exp(logs)
    return jnp.stack([jnp.sum(weights * nodes ** degree, axis=0) for degree in range(6)], axis=1)


def draw_courant_radial(key, part):
    shape = (2, LAYERS, ROWS, AZIMUTH)
    subkeys = jax.random.split(jax.random.fold_in(key, 37), 2)
    interior = jax.random.uniform(subkeys[0], shape, jnp.float32, -0.25, 0.25)
    magnitude = jax.random.uniform(subkeys[1], shape, jnp.float32, 0.15, 0.25)
    region_idx = jnp.arange(2)[:, None, None, None]
    layer_idx = jnp.arange(LAYERS)[None, :, None, None]
    rotor_edge = jnp.logical_and(region_idx == 0, layer_idx == LAYERS - 1)
    stator_edge = jnp.logical_and(region_idx == 1, layer_idx == 0)
    field = jnp.where(rotor_edge, -magnitude, interior)
    return jnp.where(stator_edge, magnitude, field)


def draw_ami_weight(key, part):
    subkeys = jax.random.split(jax.random.fold_in(key, 23), 2)
    diagonal = jax.random.uniform(subkeys[0], (2, BLOCKS, FACES), jnp.float32, 0.3, 0.7)
    spread = 0.5 / FACES
    offdiag = jax.random.uniform(subkeys[1], (2, BLOCKS, FACES, FACES), jnp.float32, 0.0, 1.0) * spread
    return offdiag + diagonal[..., None] * jnp.eye(FACES, dtype=jnp.float32)


def plant(entries, rng, smallest, high):
    longest = entries.shape.index(max(entries.shape))
    spots = []
    for shift in (0, 1):
        where = [jax.random.randint(jax.random.fold_in(rng, axis), (), 0, length) for axis, length in enumerate(entries.shape)]
        where[longest] = (where[longest] + shift) % entries.shape[longest]
        spots.append(tuple(where))
    return entries.at[spots[0]].set(smallest).at[spots[1]].set(high)


def level_of(key, shape, pieces, low, high):
    gain, own = 1.0, jax.random.fold_in(key, 6)
    for position, parts in pieces:
        heights = jnp.exp(jax.random.uniform(jax.random.fold_in(own, position), (parts,), jnp.float32, low / len(pieces), high / len(pieces)))
        gain = gain * jnp.repeat(heights, shape[position] // parts).reshape([-1 if axis == position else 1 for axis in range(len(shape))])
    return gain


def shared_out(stream_key, own, number, rows, number_of, top, limit, lean):
    ranking = jax.random.permutation(stream_key, number_of)
    heavy_load, common = shares(number_of, rows * top, limit, lean, True), shares(number_of, rows * top, limit, lean, False)
    places = jnp.arange(number_of)

    def named(tallies, turn):
        used = int((tallies > 0).sum())
        fixed = max(1, used // 4)
        passed = fixed + (places - fixed + turn * (used - fixed)) % max(1, number_of - fixed)
        return jnp.zeros((number_of,), jnp.int32).at[ranking[jnp.where(places < fixed, places, passed)]].set(jnp.asarray(tallies, jnp.int32))

    tallies = jnp.where(number % 4 == 0, named(heavy_load, number // 4), named(common, number - number // 4 - 1))
    mixed = jax.random.permutation(jax.random.fold_in(own, 3), number_of)
    donor, taker = mixed[0:number_of // 2 * 2:2], mixed[1:number_of // 2 * 2:2]
    slack = jnp.minimum(tallies[donor] - 1, limit - tallies[taker]) // 2
    slack = jnp.where((donor == ranking[0]) | (taker == ranking[0]) | (tallies[taker] == 0), 0, jnp.maximum(slack, 0))
    passed = jax.random.randint(jax.random.fold_in(own, 4), (number_of // 2,), 0, 1 << 20) % (slack + 1)
    tallies = tallies.at[donor].add(-passed).at[taker].add(passed)
    members = jnp.searchsorted(jnp.cumsum(tallies), jnp.arange(rows * top), side="right").astype(jnp.int32)
    grid = members.reshape(top, rows).T
    grid = grid[jax.random.permutation(jax.random.fold_in(own, 1), rows)]
    turn = jax.random.randint(jax.random.fold_in(own, 2), (rows, 1), 0, top)
    return jnp.take_along_axis(grid, (jnp.arange(top)[None, :] + turn) % top, axis=1)


def shares(number_of, total, most, slope, full):
    portions = [(1 << 20) // math.isqrt(rank ** slope) + 1 for rank in range(1, number_of + 1)]
    largest = most if full else min(most, max(-(-total // number_of), total * portions[0] // sum(portions)))
    least = 1 if total - largest >= number_of - 1 else 0
    counts, rest = [largest] + [least] * (number_of - 1), total - largest - least * (number_of - 1)
    while rest > 0:
        movable = [i for i in range(1, number_of) if counts[i] < largest] or [i for i in range(1, number_of) if counts[i] < most]
        whole, left = sum([portions[i] for i in movable]), rest
        for i in movable:
            extra = min(most - counts[i], max(1, left * portions[i] // whole), rest)
            counts[i] = counts[i] + extra
            rest = rest - extra
    return np.array(counts)


def setup_inputs(seed: int = 0) -> dict:
    keys = jax.random.split(jax.random.key(seed), 9)
    moments = draw_moments(jax.random.fold_in(keys[8], 71), 0)
    courant_azimuth = jnp.clip(0.1 + 0.20000001043081284 * jax.random.uniform(keys[1], (2, LAYERS, ROWS, AZIMUTH), jnp.float32) ** level_of(keys[1], (2, LAYERS, ROWS, AZIMUTH), ((0, 2), (3, 128)), -0.2, 0.2), 0.1, 0.3)
    courant_radial = draw_courant_radial(jax.random.fold_in(keys[8], 71), 0)
    courant_axial = jnp.clip(jax.random.uniform(keys[3], (2, LAYERS, ROWS, AZIMUTH), jnp.float32, -0.2, 0.2) * level_of(keys[3], (2, LAYERS, ROWS, AZIMUTH), ((0, 2), (3, 128)), -0.4, 0.0), -0.2, 0.2)
    shear = jnp.clip(jnp.exp(math.log(4.0) - 2.0794415 * jax.random.uniform(keys[4], (2, LAYERS, ROWS, AZIMUTH), jnp.float32) ** level_of(keys[4], (2, LAYERS, ROWS, AZIMUTH), ((0, 2), (3, 128)), -0.2, 0.2)), 0.5, 4.0)
    owner_keys = jax.random.split(jax.random.fold_in(keys[5], 1), 2 * BLOCKS // ROWS)
    owner_turns = jax.random.permutation(jax.random.fold_in(keys[5], 3), 2 * BLOCKS // ROWS)
    owner = jax.vmap(lambda own, number: shared_out(jax.random.fold_in(keys[5], 2), own, number, ROWS, N_CELLS, 1, CAP, 2))(owner_keys, owner_turns).reshape((2, BLOCKS, 1))
    target = plant(jax.random.randint(keys[6], (2, BLOCKS), 0, ROWS), jax.random.fold_in(keys[6], 1), 0, ROWS - 1).astype(jnp.int32)
    ami_weight = draw_ami_weight(jax.random.fold_in(keys[8], 71), 0)
    return {"moments": moments, "courant_azimuth": courant_azimuth, "courant_radial": courant_radial, "courant_axial": courant_axial, "shear": shear, "owner": owner, "target": target, "ami_weight": ami_weight}


KAGG = 0.005
KBRK = 0.02

def quadrature(moment):
    mass = moment[0]
    scaled = [moment[degree] / mass for degree in range(6)]
    mean_size = scaled[1]
    first_two = scaled[2] - mean_size * scaled[1]
    first_three = scaled[3] - mean_size * scaled[2]
    first_four = scaled[4] - mean_size * scaled[3]
    first_five = scaled[5] - mean_size * scaled[4]
    alpha_one = first_three / first_two - mean_size
    beta_one = first_two
    second_two = first_four - alpha_one * first_three - beta_one * scaled[2]
    second_three = first_five - alpha_one * first_four - beta_one * scaled[3]
    alpha_two = second_three / second_two - first_three / first_two
    beta_two = second_two / first_two
    centre = (mean_size + alpha_one + alpha_two) / 3.0
    dev_zero = mean_size - centre
    dev_one = alpha_one - centre
    dev_two = alpha_two - centre
    spread = jnp.sqrt((dev_zero * dev_zero + dev_one * dev_one + dev_two * dev_two + 2.0 * (beta_one + beta_two)) / 6.0)
    determ = dev_zero * (dev_one * dev_two - beta_two) - beta_one * dev_two
    cosine = jnp.clip(determ / (2.0 * spread * spread * spread), -1.0, 1.0)
    third = jnp.arccos(cosine) / 3.0
    node_high = centre + 2.0 * spread * jnp.cos(third)
    node_low = centre + 2.0 * spread * jnp.cos(third + 2.0 * math.pi / 3.0)
    node_mid = 3.0 * centre - node_high - node_low
    nodes = [node_low, node_mid, node_high]
    weights = []
    for node in nodes:
        lead = node - mean_size
        trail = (node - alpha_one) * lead - beta_one
        norm_sq = 1.0 + lead * lead / beta_one + trail * trail / (beta_one * beta_two)
        weights.append(mass / norm_sq)
    return (nodes, weights)

def sources(moment, shear):
    nodes, weights = quadrature(moment)
    cubes = [node * node * node for node in nodes]
    pairs = []
    for first in range(3):
        for second in range(3):
            summed = nodes[first] + nodes[second]
            kernel = shear * summed * summed * summed
            pairs.append((first, second, weights[first] * weights[second] * kernel, jnp.log(cubes[first] + cubes[second])))
    result = []
    for degree in range(6):
        birth = jnp.zeros_like(shear)
        death = jnp.zeros_like(shear)
        for first, second, pair, logsum in pairs:
            birth = birth + 0.5 * pair * jnp.exp(degree / 3.0 * logsum)
            death = death + pair * nodes[first] ** degree
        factor = 2.0 ** (1.0 - degree / 3.0) - 1.0
        breakage = jnp.zeros_like(shear)
        for index in range(3):
            breakage = breakage + weights[index] * KBRK * shear * cubes[index] * factor * nodes[index] ** degree
        result.append(moment[degree] + KAGG * (birth - death) + breakage)
    return jnp.stack(result)

def advance(moment, previous, ghost_layer, is_rotor, azim, radial, axial, shear):
    empty_layer = jnp.zeros_like(ghost_layer)
    beyond_edge = jnp.where(is_rotor, ghost_layer, empty_layer)
    below_edge = jnp.where(is_rotor, empty_layer, ghost_layer)
    prev_azim = jnp.concatenate([previous[..., None], moment[..., :-1]], axis=3)
    radial_below = jnp.concatenate([below_edge[:, None], moment[:, :-1]], axis=1)
    radial_beyond = jnp.concatenate([moment[:, 1:], beyond_edge[:, None]], axis=1)
    axial_pad = jnp.zeros_like(moment[:, :, :1])
    axial_below = jnp.concatenate([axial_pad, moment[:, :, :-1]], axis=2)
    axial_beyond = jnp.concatenate([moment[:, :, 1:], axial_pad], axis=2)
    advected = moment - azim * (moment - prev_azim) - jnp.maximum(radial, 0.0) * (moment - radial_below) - jnp.minimum(radial, 0.0) * (radial_beyond - moment) - jnp.maximum(axial, 0.0) * (moment - axial_below) - jnp.minimum(axial, 0.0) * (axial_beyond - moment)
    return sources([advected[degree] for degree in range(6)], shear)

def reference(moments, courant_azimuth, courant_radial, courant_axial, shear, owner, target, ami_weight):
    groups = 2 * N_CELLS
    blocked = moments.reshape(2, 6, LAYERS, ROWS, N_CELLS, FACES).transpose(0, 4, 1, 2, 3, 5).reshape(groups, 6, LAYERS, ROWS, FACES)

    def split_field(field):
        return field.reshape(2, LAYERS, ROWS, N_CELLS, FACES).transpose(0, 3, 1, 2, 4).reshape(groups, LAYERS, ROWS, FACES)
    azim_b = split_field(courant_azimuth)
    radial_b = split_field(courant_radial)
    axial_b = split_field(courant_axial)
    shear_b = split_field(shear)
    rotor_flags = jnp.arange(groups) < N_CELLS
    layers = jnp.where(rotor_flags[:, None, None, None], blocked[:, :, LAYERS - 1], blocked[:, :, 0])
    weights_b = ami_weight.reshape(groups, ROWS, FACES, FACES)

    def weigh(pair):
        return jnp.einsum('zfg,kzg->zkf', pair[0], pair[1], precision=lax.Precision.HIGHEST)
    contrib = lax.map(weigh, (weights_b, layers)).reshape(2, N_CELLS * ROWS, 6, FACES)
    dest = owner[:, :, 0] * ROWS + target
    empty = jnp.zeros((N_CELLS * ROWS, 6, FACES), jnp.float32)
    ghost_rotor = empty.at[dest[1]].add(contrib[1])
    ghost_stator = empty.at[dest[0]].add(contrib[0])
    ghost = jnp.stack([ghost_rotor, ghost_stator]).reshape(2, N_CELLS, ROWS, 6, FACES).transpose(0, 1, 3, 2, 4).reshape(groups, 6, ROWS, FACES)
    rims = blocked[..., FACES - 1].reshape(2, N_CELLS, 6, LAYERS, ROWS)
    rims = jnp.roll(rims, 1, axis=1).reshape(groups, 6, LAYERS, ROWS)

    def step_block(items):
        return advance(items[0], items[1], items[2], items[3], items[4], items[5], items[6], items[7])
    updated = lax.map(step_block, (blocked, rims, ghost, rotor_flags, azim_b, radial_b, axial_b, shear_b))
    return updated.reshape(2, N_CELLS, 6, LAYERS, ROWS, FACES).transpose(0, 2, 3, 4, 1, 5).reshape(2, 6, LAYERS, ROWS, N_CELLS * FACES)
```

```python
import functools

import jax
import jax.numpy as jnp
from jax import lax
from jax.experimental import pallas as pl
from jax.experimental.pallas import tpu as pltpu
from jax.sharding import PartitionSpec as P

MESH = pl.DeviceIdType.MESH
F32 = jnp.float32
BF16 = jnp.bfloat16
KAGG = 0.005
KBRK = 0.02
LAYERS = 4
ROWS = 128
FACES = 128
MOMENTS = 6
PEERS = 128
SLOTS = 2
MESSAGE = SLOTS * MOMENTS + 1
PLANE = ROWS + 16
CHUNKS = 8
BLOCK = 16
CUBE_ROOT_2 = 2.0 ** (1.0 / 3.0)

THIRD_ANGLE = (
    0.5000000032577528,
    0.5773497198231888,
    -0.11109568329657703,
    0.053288656003267744,
    -0.03196129546407778,
    0.019675718215576045,
    -0.01032549308338918,
    0.003707686483927317,
    -0.0006393143691536856,
)


def third_angle(s):
    value = THIRD_ANGLE[-1] * s + THIRD_ANGLE[-2]
    for coefficient in THIRD_ANGLE[-3::-1]:
        value = value * s + coefficient
    return value


def quadrature(moment):
    mass = moment[0]
    inverse = 1.0 / mass
    n1, n2, n3, n4, n5 = [moment[degree] * inverse for degree in range(1, 6)]
    a0 = n1
    p1 = n2 - a0 * n1
    p2 = n3 - a0 * n2
    p3 = n4 - a0 * n3
    p4 = n5 - a0 * n4
    over_p1 = 1.0 / p1
    ratio = p2 * over_p1
    a1 = ratio - a0
    q2 = p3 - a1 * p2 - p1 * n2
    q3 = p4 - a1 * p3 - p1 * n3
    over_q2 = 1.0 / q2
    a2 = q3 * over_q2 - ratio
    b2 = q2 * over_p1
    centre = (a0 + a1 + a2) * (1.0 / 3.0)
    d0 = a0 - centre
    d1 = a1 - centre
    d2 = a2 - centre
    square = (d0 * d0 + d1 * d1 + d2 * d2 + 2.0 * (p1 + b2)) * (1.0 / 6.0)
    over_h = lax.rsqrt(square)
    h2 = 2.0 * square * over_h
    determ = d0 * (d1 * d2 - b2) - p1 * d2
    half_cosine = jnp.clip(0.25 * determ * (over_h * over_h * over_h), -0.5, 0.5)
    high = centre + h2 * third_angle(jnp.sqrt(0.5 + half_cosine))
    low = centre - h2 * third_angle(jnp.sqrt(0.5 - half_cosine))
    middle = 3.0 * centre - high - low
    nodes = [low, middle, high]
    weights = []
    for node in nodes:
        lead = node - a0
        trail = (node - a1) * lead - p1
        weights.append(mass / (1.0 + lead * lead * over_p1 + trail * trail * over_q2))
    return nodes, weights


def sources(moment, shear):
    nodes, weights = quadrature(moment)
    cubes = [node * node * node for node in nodes]
    merge = KAGG * shear
    split = KBRK * shear
    carried = [w * c for w, c in zip(weights, cubes)]
    born = [4.0 * w * a * merge for w, a in zip(weights, carried)]
    broken = [split * a for a in carried]
    lost = [2.0 * b + f for b, f in zip(born, broken)]
    terms, steps = [], []
    for first, second in ((0, 1), (0, 2), (1, 2)):
        summed = nodes[first] + nodes[second]
        pair = merge * (weights[first] * weights[second]) * (summed * summed * summed)
        lost[first] = lost[first] + pair
        lost[second] = lost[second] + pair
        terms.append(pair)
        steps.append(jnp.exp(jnp.log(cubes[first] + cubes[second]) * (1.0 / 3.0)))
    for index in range(3):
        terms += [born[index], 2.0 * broken[index], -lost[index]]
        node = nodes[index]
        steps += [CUBE_ROOT_2 * node, (1.0 / CUBE_ROOT_2) * node, node]
    result = []
    for degree in range(MOMENTS):
        if degree:
            terms = [term * step for term, step in zip(terms, steps)]
        total = moment[degree]
        for term in terms:
            total = total + term
        result.append(total)
    return result


def kernel(
    moments_hbm,
    azimuth_hbm,
    radial_hbm,
    axial_hbm,
    shear_hbm,
    owner_hbm,
    target_hbm,
    weight_hbm,
    out_ref,
    cells,
    azimuth,
    radial,
    axial,
    shear,
    owner,
    target,
    weight,
    face,
    contrib,
    index_vmem,
    index_smem,
    outgoing,
    incoming,
    rim_out,
    rim_in,
    small_sem,
    cell_sem,
    weight_sem,
    send_sem,
    recv_sem,
    rim_send_sem,
    rim_recv_sem,
):
    region = lax.axis_index("region")
    me = lax.axis_index("cells")
    other = 1 - region
    after = lax.rem(me + 1, PEERS)
    before = lax.rem(me + PEERS - 1, PEERS)
    interface = (LAYERS - 1) * other
    per_chunk = ROWS // CHUNKS

    def plane(k, layer):
        return (k * (LAYERS + 2) + layer) * PLANE

    small = [
        pltpu.make_async_copy(owner_hbm, owner, small_sem.at[0]),
        pltpu.make_async_copy(target_hbm, target, small_sem.at[1]),
    ]
    for copy in small:
        copy.start()
    faces = [
        pltpu.make_async_copy(
            moments_hbm.at[k, interface], face.at[pl.ds(k * ROWS, ROWS)], cell_sem.at[k]
        )
        for k in range(MOMENTS)
    ]
    for copy in faces:
        copy.start()
    chunks = [
        pltpu.make_async_copy(
            weight_hbm.at[pl.ds(c * per_chunk * FACES, per_chunk * FACES)],
            weight.at[pl.ds(c * per_chunk * FACES, per_chunk * FACES)],
            weight_sem.at[c],
        )
        for c in range(CHUNKS)
    ]
    body_copies = []
    for k in range(MOMENTS):
        for layer in range(LAYERS):
            body_copies.append(
                pltpu.make_async_copy(
                    moments_hbm.at[k, layer],
                    cells.at[pl.ds(plane(k, layer + 1) + 8, ROWS)],
                    cell_sem.at[MOMENTS + k * LAYERS + layer],
                )
            )
    fields = [
        pltpu.make_async_copy(source, destination, small_sem.at[2 + i])
        for i, (source, destination) in enumerate(
            ((azimuth_hbm, azimuth), (radial_hbm, radial), (axial_hbm, axial), (shear_hbm, shear))
        )
    ]
    for c in range(CHUNKS - 2):
        chunks[c].start()
    for copy in body_copies:
        copy.start()
    for c in range(CHUNKS - 2, CHUNKS):
        chunks[c].start()
    for copy in fields:
        copy.start()

    barrier = pltpu.get_barrier_semaphore()

    def greet(peer, carry):
        pl.semaphore_signal(barrier, inc=1, device_id=(other, peer), device_id_type=MESH)
        return carry

    lax.fori_loop(0, PEERS, greet, 0, unroll=8)
    for peer in (after, before):
        pl.semaphore_signal(barrier, inc=1, device_id=(region, peer), device_id_type=MESH)

    for copy in small:
        copy.wait()
    square = (ROWS, PEERS)
    sublane = lax.broadcasted_iota(jnp.int32, square, 0)
    lane = lax.broadcasted_iota(jnp.int32, square, 1)
    by_lane = jnp.broadcast_to(owner[...], square)
    by_sublane = by_lane.T
    same = by_lane == by_sublane
    rank_row = jnp.sum(jnp.where(same & (sublane < lane), 1, 0), axis=0, keepdims=True)
    rank_column = jnp.sum(jnp.where(same & (lane < sublane), 1, 0), axis=1, keepdims=True)
    target_row = jnp.broadcast_to(target[...].astype(F32), square)
    meta = jnp.zeros(square, F32)
    index_vmem[...] = jnp.zeros(index_vmem.shape, jnp.int32)
    for r in range(SLOTS):
        chosen = (by_sublane == lane) & (rank_column == r)
        index = ROWS + jnp.sum(jnp.where(chosen, sublane - ROWS, 0), axis=0, keepdims=True)
        index_vmem[r : r + 1, :] = index
        chosen = (by_lane == sublane) & (rank_row == r)
        row = jnp.sum(jnp.where(chosen, target_row, 0.0), axis=1, keepdims=True)
        meta = jnp.where(lane == r, row, meta)
    outgoing[pl.ds(MESSAGE - 1, PEERS, stride=MESSAGE), :] = meta
    to_scalar = pltpu.make_async_copy(index_vmem, index_smem, small_sem.at[6])
    to_scalar.start()

    contrib[ROWS] = jnp.zeros((8, FACES), F32)
    for copy in faces:
        copy.wait()

    def weigh(z, carry):
        source = face[pl.ds(z, MOMENTS, stride=ROWS), :]
        source = jnp.concatenate([source, jnp.zeros((2, FACES), F32)], axis=0)
        source_high = source.astype(BF16).astype(F32)
        both = jnp.concatenate([source_high, source - source_high], axis=0).astype(BF16)
        matrix = weight[pl.ds(pl.multiple_of(z * FACES, FACES), FACES), :]
        high = matrix.astype(BF16)
        low = (matrix - high.astype(F32)).astype(BF16)
        product = lax.dot_general(
            both,
            jnp.concatenate([high, low], axis=0),
            (((1,), (1,)), ((), ())),
            preferred_element_type=F32,
        )
        contrib[z] = (
            product[:8, :FACES] + (product[8:, :FACES] + product[:8, FACES:])
        )
        return carry

    for c in range(CHUNKS - 2):
        chunks[c].wait()
        lax.fori_loop(c * per_chunk, (c + 1) * per_chunk, weigh, 0, unroll=4)

    for copy in body_copies:
        copy.wait()
    zero_rows = jnp.zeros((8, FACES), F32)

    def edges(i, carry):
        base = pl.multiple_of(i * PLANE, 8)
        cells[pl.ds(base, 8), :] = zero_rows
        cells[pl.ds(base + 8 + ROWS, 8), :] = zero_rows
        return carry

    lax.fori_loop(0, MOMENTS * (LAYERS + 2), edges, 0)
    for k in range(MOMENTS):
        empty = plane(k, (LAYERS + 1) * region)
        cells[pl.ds(empty + 8, ROWS), :] = jnp.zeros((ROWS, FACES), F32)

    lanes = lax.broadcasted_iota(jnp.int32, (8, FACES), 1)

    def pack(i, carry):
        packed = jnp.zeros((8, FACES), F32)
        for k in range(MOMENTS):
            for layer in range(LAYERS):
                p = k * LAYERS + layer
                values = cells[pl.ds(pl.multiple_of(plane(k, layer + 1) + 8 + i * 8, 8), 8), :]
                packed = jnp.where(lanes == p, pltpu.roll(values, p + 1, 1), packed)
        rim_out[pl.ds(pl.multiple_of(i * 8, 8), 8), :] = packed
        return carry

    lax.fori_loop(0, ROWS // 8, pack, 0)
    for c in range(CHUNKS - 2, CHUNKS):
        chunks[c].wait()
        lax.fori_loop(c * per_chunk, (c + 1) * per_chunk, weigh, 0, unroll=4)
    to_scalar.wait()

    pl.semaphore_wait(barrier, PEERS + 2)
    rim = pltpu.make_async_remote_copy(
        src_ref=rim_out,
        dst_ref=rim_in,
        send_sem=rim_send_sem,
        recv_sem=rim_recv_sem,
        device_id=(region, after),
        device_id_type=MESH,
    )
    rim.start()

    def dispatch(peer, carry):
        for r in range(SLOTS):
            block = index_smem[r, peer]
            values = contrib[block]
            outgoing[pl.ds(MESSAGE * peer + MOMENTS * r, MOMENTS), :] = values[:MOMENTS]
        pltpu.make_async_remote_copy(
            src_ref=outgoing.at[pl.ds(MESSAGE * peer, MESSAGE)],
            dst_ref=incoming.at[pl.ds(MESSAGE * me, MESSAGE)],
            send_sem=send_sem,
            recv_sem=recv_sem,
            device_id=(other, peer),
            device_id_type=MESH,
        ).start()
        return carry

    lax.fori_loop(0, PEERS, dispatch, 0, unroll=2)

    for copy in fields:
        copy.wait()
    rim.wait_recv()
    lanes_block = lax.broadcasted_iota(jnp.int32, (BLOCK, FACES), 1)

    def layer_step(layer, i):
        start = pl.multiple_of(i * BLOCK, BLOCK)
        at = pl.multiple_of(layer * ROWS + start, BLOCK)
        ca = azimuth[pl.ds(at, BLOCK), :]
        cr = radial[pl.ds(at, BLOCK), :]
        cz = axial[pl.ds(at, BLOCK), :]
        outward = cr > 0.0
        upward = cz > 0.0
        cr = jnp.abs(cr)
        cz = jnp.abs(cz)
        keep = 1.0 - ca - cr - cz
        rims = rim_in[pl.ds(start, BLOCK), :]
        advected = []
        for k in range(MOMENTS):
            row = plane(k, layer + 1) + 8 + start
            m = cells[pl.ds(row, BLOCK), :]
            shift = lax.rem(2 * FACES - (k * LAYERS + layer), FACES)
            previous = jnp.where(
                lanes_block == 0, pltpu.roll(rims, shift, 1), pltpu.roll(m, 1, 1)
            )
            below = cells[pl.ds(row - PLANE, BLOCK), :]
            beyond = cells[pl.ds(row + PLANE, BLOCK), :]
            axial_below = cells[pl.ds(row - 1, BLOCK), :]
            axial_beyond = cells[pl.ds(row + 1, BLOCK), :]
            advected.append(
                keep * m
                + ca * previous
                + cr * jnp.where(outward, below, beyond)
                + cz * jnp.where(upward, axial_below, axial_beyond)
            )
        result = sources(advected, shear[pl.ds(at, BLOCK), :])
        for k in range(MOMENTS):
            out_ref[k, layer, pl.ds(start, BLOCK), :] = result[k]

    def inner(n, carry):
        layer = region + n // (ROWS // BLOCK)
        layer_step(layer, lax.rem(n, ROWS // BLOCK))
        return carry

    lax.fori_loop(0, (LAYERS - 1) * (ROWS // BLOCK), inner, 0)

    whole = pltpu.make_async_remote_copy(
        src_ref=outgoing,
        dst_ref=incoming,
        send_sem=send_sem,
        recv_sem=recv_sem,
        device_id=(other, me),
        device_id_type=MESH,
    )
    whole.wait_recv()

    meta = incoming[pl.ds(MESSAGE - 1, PEERS, stride=MESSAGE), :]
    hits = jnp.concatenate(
        [jnp.where(meta[:, r : r + 1] == lane.astype(F32), 1.0, 0.0).T for r in range(SLOTS)], axis=1
    ).astype(BF16)
    ghost_layer = (LAYERS + 1) * other
    for k in range(MOMENTS):
        received = jnp.concatenate(
            [
                incoming[pl.ds(r * MOMENTS + k, PEERS, stride=MESSAGE), :]
                for r in range(SLOTS)
            ],
            axis=0,
        )
        high = received.astype(BF16)
        low = (received - high.astype(F32)).astype(BF16)
        summed = jnp.dot(
            hits, jnp.concatenate([high, low], axis=1), preferred_element_type=F32
        )
        cells[pl.ds(plane(k, ghost_layer) + 8, ROWS), :] = summed[:, :FACES] + summed[:, FACES:]

    def outer(i, carry):
        layer_step(interface, i)
        return carry

    lax.fori_loop(0, ROWS // BLOCK, outer, 0)
    whole.wait_send()
    rim.wait_send()


def on_device(
    moments, courant_azimuth, courant_radial, courant_axial, shear, owner, target, ami_weight
):
    shape = (MOMENTS, LAYERS, ROWS, FACES)
    field = (LAYERS * ROWS, FACES)
    dma = pltpu.SemaphoreType.DMA
    updated = pl.pallas_call(
        kernel,
        out_shape=jax.ShapeDtypeStruct(shape, F32),
        in_specs=[pl.BlockSpec(memory_space=pl.ANY)] * 8,
        out_specs=pl.BlockSpec(memory_space=pltpu.VMEM),
        scratch_shapes=[
            pltpu.VMEM((MOMENTS * (LAYERS + 2) * PLANE, FACES), F32),
            pltpu.VMEM(field, F32),
            pltpu.VMEM(field, F32),
            pltpu.VMEM(field, F32),
            pltpu.VMEM(field, F32),
            pltpu.VMEM((1, ROWS), jnp.int32),
            pltpu.VMEM((1, ROWS), jnp.int32),
            pltpu.VMEM((ROWS * FACES, FACES), F32),
            pltpu.VMEM((MOMENTS * ROWS, FACES), F32),
            pltpu.VMEM((ROWS + 1, 8, FACES), F32),
            pltpu.VMEM((8, PEERS), jnp.int32),
            pltpu.SMEM((8, PEERS), jnp.int32),
            pltpu.VMEM((MESSAGE * PEERS, FACES), F32),
            pltpu.VMEM((MESSAGE * PEERS, FACES), F32),
            pltpu.VMEM((ROWS, FACES), F32),
            pltpu.VMEM((ROWS, FACES), F32),
            dma((7,)),
            dma((MOMENTS + MOMENTS * LAYERS,)),
            dma((CHUNKS,)),
            dma,
            dma,
            dma,
            dma,
        ],
        compiler_params=pltpu.CompilerParams(
            collective_id=0, has_side_effects=True, vmem_limit_bytes=48 * 1024 * 1024
        ),
        name="transport",
    )(
        moments.reshape(shape),
        courant_azimuth.reshape(field),
        courant_radial.reshape(field),
        courant_axial.reshape(field),
        shear.reshape(field),
        owner.reshape(1, ROWS),
        target.reshape(1, ROWS),
        ami_weight.reshape(ROWS * FACES, FACES),
    )
    return updated[None]


def solution(mesh):
    placed = (
        P("region", None, None, None, "cells"),
        P("region", None, None, "cells"),
        P("region", None, None, "cells"),
        P("region", None, None, "cells"),
        P("region", None, None, "cells"),
        P("region", "cells", None),
        P("region", "cells"),
        P("region", "cells", None, None),
    )
    return jax.shard_map(
        on_device,
        mesh=mesh,
        in_specs=placed,
        out_specs=P("region", None, None, None, "cells"),
        check_vma=False,
    )
```

```python
import functools

import jax
import jax.numpy as jnp
from jax import lax
from jax.experimental import pallas as pl
from jax.experimental.pallas import tpu as pltpu
from jax.sharding import PartitionSpec as P

MESH = pl.DeviceIdType.MESH
F32 = jnp.float32
BF16 = jnp.bfloat16
KAGG = 0.005
KBRK = 0.02
LAYERS = 4
ROWS = 128
FACES = 128
MOMENTS = 6
PEERS = 128
SLOTS = 2
MESSAGE = SLOTS * MOMENTS + 1
PLANE = ROWS + 16
CHUNKS = 8
BLOCK = 16
CUBE_ROOT_2 = 2.0 ** (1.0 / 3.0)

THIRD_ANGLE = (
    0.5000000032577528,
    0.5773497198231888,
    -0.11109568329657703,
    0.053288656003267744,
    -0.03196129546407778,
    0.019675718215576045,
    -0.01032549308338918,
    0.003707686483927317,
    -0.0006393143691536856,
)


def third_angle(s):
    value = THIRD_ANGLE[-1] * s + THIRD_ANGLE[-2]
    for coefficient in THIRD_ANGLE[-3::-1]:
        value = value * s + coefficient
    return value


def quadrature(moment):
    mass = moment[0]
    inverse = 1.0 / mass
    n1, n2, n3, n4, n5 = [moment[degree] * inverse for degree in range(1, 6)]
    a0 = n1
    p1 = n2 - a0 * n1
    p2 = n3 - a0 * n2
    p3 = n4 - a0 * n3
    p4 = n5 - a0 * n4
    over_p1 = 1.0 / p1
    ratio = p2 * over_p1
    a1 = ratio - a0
    q2 = p3 - a1 * p2 - p1 * n2
    q3 = p4 - a1 * p3 - p1 * n3
    over_q2 = 1.0 / q2
    a2 = q3 * over_q2 - ratio
    b2 = q2 * over_p1
    centre = (a0 + a1 + a2) * (1.0 / 3.0)
    d0 = a0 - centre
    d1 = a1 - centre
    d2 = a2 - centre
    square = (d0 * d0 + d1 * d1 + d2 * d2 + 2.0 * (p1 + b2)) * (1.0 / 6.0)
    over_h = lax.rsqrt(square)
    h2 = 2.0 * square * over_h
    determ = d0 * (d1 * d2 - b2) - p1 * d2
    half_cosine = jnp.clip(0.25 * determ * (over_h * over_h * over_h), -0.5, 0.5)
    high = centre + h2 * third_angle(jnp.sqrt(0.5 + half_cosine))
    low = centre - h2 * third_angle(jnp.sqrt(0.5 - half_cosine))
    middle = 3.0 * centre - high - low
    nodes = [low, middle, high]
    weights = []
    for node in nodes:
        lead = node - a0
        trail = (node - a1) * lead - p1
        weights.append(mass / (1.0 + lead * lead * over_p1 + trail * trail * over_q2))
    return nodes, weights


def sources(moment, shear):
    nodes, weights = quadrature(moment)
    cubes = [node * node * node for node in nodes]
    merge = KAGG * shear
    split = KBRK * shear
    carried = [w * c for w, c in zip(weights, cubes)]
    born = [4.0 * w * a * merge for w, a in zip(weights, carried)]
    broken = [split * a for a in carried]
    lost = [2.0 * b + f for b, f in zip(born, broken)]
    terms, steps = [], []
    for first, second in ((0, 1), (0, 2), (1, 2)):
        summed = nodes[first] + nodes[second]
        pair = merge * (weights[first] * weights[second]) * (summed * summed * summed)
        lost[first] = lost[first] + pair
        lost[second] = lost[second] + pair
        terms.append(pair)
        steps.append(jnp.exp(jnp.log(cubes[first] + cubes[second]) * (1.0 / 3.0)))
    for index in range(3):
        terms += [born[index], 2.0 * broken[index], -lost[index]]
        node = nodes[index]
        steps += [CUBE_ROOT_2 * node, (1.0 / CUBE_ROOT_2) * node, node]
    result = []
    for degree in range(MOMENTS):
        if degree:
            terms = [term * step for term, step in zip(terms, steps)]
        total = moment[degree]
        for term in terms:
            total = total + term
        result.append(total)
    return result


def kernel(
    moments_hbm,
    azimuth_hbm,
    radial_hbm,
    axial_hbm,
    shear_hbm,
    owner_hbm,
    target_hbm,
    weight_hbm,
    out_ref,
    cells,
    azimuth,
    radial,
    axial,
    shear,
    owner,
    target,
    weight,
    face,
    contrib,
    index_vmem,
    index_smem,
    outgoing,
    incoming,
    rim_out,
    rim_in,
    small_sem,
    cell_sem,
    weight_sem,
    send_sem,
    recv_sem,
    rim_send_sem,
    rim_recv_sem,
):
    region = lax.axis_index("region")
    me = lax.axis_index("cells")
    other = 1 - region
    after = lax.rem(me + 1, PEERS)
    before = lax.rem(me + PEERS - 1, PEERS)
    interface = (LAYERS - 1) * other
    per_chunk = ROWS // CHUNKS

    def plane(k, layer):
        return (k * (LAYERS + 2) + layer) * PLANE

    small = [
        pltpu.make_async_copy(owner_hbm, owner, small_sem.at[0]),
        pltpu.make_async_copy(target_hbm, target, small_sem.at[1]),
    ]
    for copy in small:
        copy.start()
    faces = [
        pltpu.make_async_copy(
            moments_hbm.at[k, interface], face.at[pl.ds(k * ROWS, ROWS)], cell_sem.at[k]
        )
        for k in range(MOMENTS)
    ]
    for copy in faces:
        copy.start()
    chunks = [
        pltpu.make_async_copy(
            weight_hbm.at[pl.ds(c * per_chunk * FACES, per_chunk * FACES)],
            weight.at[pl.ds(c * per_chunk * FACES, per_chunk * FACES)],
            weight_sem.at[c],
        )
        for c in range(CHUNKS)
    ]
    body_copies = []
    for k in range(MOMENTS):
        for layer in range(LAYERS):
            body_copies.append(
                pltpu.make_async_copy(
                    moments_hbm.at[k, layer],
                    cells.at[pl.ds(plane(k, layer + 1) + 8, ROWS)],
                    cell_sem.at[MOMENTS + k * LAYERS + layer],
                )
            )
    fields = [
        pltpu.make_async_copy(source, destination, small_sem.at[2 + i])
        for i, (source, destination) in enumerate(
            ((azimuth_hbm, azimuth), (radial_hbm, radial), (axial_hbm, axial), (shear_hbm, shear))
        )
    ]
    for c in range(CHUNKS - 2):
        chunks[c].start()
    for copy in body_copies:
        copy.start()
    for c in range(CHUNKS - 2, CHUNKS):
        chunks[c].start()
    for copy in fields:
        copy.start()

    barrier = pltpu.get_barrier_semaphore()

    def greet(peer, carry):
        pl.semaphore_signal(barrier, inc=1, device_id=(other, peer), device_id_type=MESH)
        return carry

    lax.fori_loop(0, PEERS, greet, 0, unroll=8)
    for peer in (after, before):
        pl.semaphore_signal(barrier, inc=1, device_id=(region, peer), device_id_type=MESH)

    for copy in small:
        copy.wait()
    square = (ROWS, PEERS)
    sublane = lax.broadcasted_iota(jnp.int32, square, 0)
    lane = lax.broadcasted_iota(jnp.int32, square, 1)
    by_lane = jnp.broadcast_to(owner[...], square)
    by_sublane = by_lane.T
    same = by_lane == by_sublane
    rank_row = jnp.sum(jnp.where(same & (sublane < lane), 1, 0), axis=0, keepdims=True)
    rank_column = jnp.sum(jnp.where(same & (lane < sublane), 1, 0), axis=1, keepdims=True)
    target_row = jnp.broadcast_to(target[...].astype(F32), square)
    meta = jnp.zeros(square, F32)
    index_vmem[...] = jnp.zeros(index_vmem.shape, jnp.int32)
    for r in range(SLOTS):
        chosen = (by_sublane == lane) & (rank_column == r)
        index = ROWS + jnp.sum(jnp.where(chosen, sublane - ROWS, 0), axis=0, keepdims=True)
        index_vmem[r : r + 1, :] = index
        chosen = (by_lane == sublane) & (rank_row == r)
        row = jnp.sum(jnp.where(chosen, target_row, 0.0), axis=1, keepdims=True)
        meta = jnp.where(lane == r, row, meta)
    outgoing[pl.ds(MESSAGE - 1, PEERS, stride=MESSAGE), :] = meta
    to_scalar = pltpu.make_async_copy(index_vmem, index_smem, small_sem.at[6])
    to_scalar.start()

    contrib[ROWS] = jnp.zeros((8, FACES), F32)
    for copy in faces:
        copy.wait()

    def weigh(z, carry):
        source = face[pl.ds(z, MOMENTS, stride=ROWS), :]
        source = jnp.concatenate([source, jnp.zeros((2, FACES), F32)], axis=0)
        source_high = source.astype(BF16).astype(F32)
        both = jnp.concatenate([source_high, source - source_high], axis=0).astype(BF16)
        matrix = weight[pl.ds(pl.multiple_of(z * FACES, FACES), FACES), :]
        high = matrix.astype(BF16)
        low = (matrix - high.astype(F32)).astype(BF16)
        product = lax.dot_general(
            both,
            jnp.concatenate([high, low], axis=0),
            (((1,), (1,)), ((), ())),
            preferred_element_type=F32,
        )
        contrib[z] = (
            product[:8, :FACES] + (product[8:, :FACES] + product[:8, FACES:])
        )
        return carry

    for c in range(CHUNKS - 2):
        chunks[c].wait()
        lax.fori_loop(c * per_chunk, (c + 1) * per_chunk, weigh, 0, unroll=per_chunk)

    for copy in body_copies:
        copy.wait()
    zero_rows = jnp.zeros((8, FACES), F32)

    def edges(i, carry):
        base = pl.multiple_of(i * PLANE, 8)
        cells[pl.ds(base, 8), :] = zero_rows
        cells[pl.ds(base + 8 + ROWS, 8), :] = zero_rows
        return carry

    lax.fori_loop(0, MOMENTS * (LAYERS + 2), edges, 0)
    for k in range(MOMENTS):
        empty = plane(k, (LAYERS + 1) * region)
        cells[pl.ds(empty + 8, ROWS), :] = jnp.zeros((ROWS, FACES), F32)

    lanes = lax.broadcasted_iota(jnp.int32, (8, FACES), 1)

    def pack(i, carry):
        packed = jnp.zeros((8, FACES), F32)
        for k in range(MOMENTS):
            for layer in range(LAYERS):
                p = k * LAYERS + layer
                values = cells[pl.ds(pl.multiple_of(plane(k, layer + 1) + 8 + i * 8, 8), 8), :]
                packed = jnp.where(lanes == p, pltpu.roll(values, p + 1, 1), packed)
        rim_out[pl.ds(pl.multiple_of(i * 8, 8), 8), :] = packed
        return carry

    lax.fori_loop(0, ROWS // 8, pack, 0)
    for c in range(CHUNKS - 2, CHUNKS):
        chunks[c].wait()
        lax.fori_loop(c * per_chunk, (c + 1) * per_chunk, weigh, 0, unroll=per_chunk)
    to_scalar.wait()

    pl.semaphore_wait(barrier, PEERS + 2)
    rim = pltpu.make_async_remote_copy(
        src_ref=rim_out,
        dst_ref=rim_in,
        send_sem=rim_send_sem,
        recv_sem=rim_recv_sem,
        device_id=(region, after),
        device_id_type=MESH,
    )
    rim.start()

    def dispatch(peer, carry):
        for r in range(SLOTS):
            block = index_smem[r, peer]
            values = contrib[block]
            outgoing[pl.ds(MESSAGE * peer + MOMENTS * r, MOMENTS), :] = values[:MOMENTS]
        pltpu.make_async_remote_copy(
            src_ref=outgoing.at[pl.ds(MESSAGE * peer, MESSAGE)],
            dst_ref=incoming.at[pl.ds(MESSAGE * me, MESSAGE)],
            send_sem=send_sem,
            recv_sem=recv_sem,
            device_id=(other, peer),
            device_id_type=MESH,
        ).start()
        return carry

    lax.fori_loop(0, PEERS, dispatch, 0, unroll=2)

    for copy in fields:
        copy.wait()
    rim.wait_recv()
    lanes_block = lax.broadcasted_iota(jnp.int32, (BLOCK, FACES), 1)

    def layer_step(layer, i):
        start = pl.multiple_of(i * BLOCK, BLOCK)
        at = pl.multiple_of(layer * ROWS + start, BLOCK)
        ca = azimuth[pl.ds(at, BLOCK), :]
        cr = radial[pl.ds(at, BLOCK), :]
        cz = axial[pl.ds(at, BLOCK), :]
        outward = cr > 0.0
        upward = cz > 0.0
        cr = jnp.abs(cr)
        cz = jnp.abs(cz)
        keep = 1.0 - ca - cr - cz
        rims = rim_in[pl.ds(start, BLOCK), :]
        advected = []
        for k in range(MOMENTS):
            row = plane(k, layer + 1) + 8 + start
            m = cells[pl.ds(row, BLOCK), :]
            shift = lax.rem(2 * FACES - (k * LAYERS + layer), FACES)
            previous = jnp.where(
                lanes_block == 0, pltpu.roll(rims, shift, 1), pltpu.roll(m, 1, 1)
            )
            below = cells[pl.ds(row - PLANE, BLOCK), :]
            beyond = cells[pl.ds(row + PLANE, BLOCK), :]
            axial_below = cells[pl.ds(row - 1, BLOCK), :]
            axial_beyond = cells[pl.ds(row + 1, BLOCK), :]
            advected.append(
                keep * m
                + ca * previous
                + cr * jnp.where(outward, below, beyond)
                + cz * jnp.where(upward, axial_below, axial_beyond)
            )
        result = sources(advected, shear[pl.ds(at, BLOCK), :])
        for k in range(MOMENTS):
            out_ref[k, layer, pl.ds(start, BLOCK), :] = result[k]

    def inner(n, carry):
        layer = region + n // (ROWS // BLOCK)
        layer_step(layer, lax.rem(n, ROWS // BLOCK))
        return carry

    lax.fori_loop(0, (LAYERS - 1) * (ROWS // BLOCK), inner, 0)

    whole = pltpu.make_async_remote_copy(
        src_ref=outgoing,
        dst_ref=incoming,
        send_sem=send_sem,
        recv_sem=recv_sem,
        device_id=(other, me),
        device_id_type=MESH,
    )
    whole.wait_recv()

    meta = incoming[pl.ds(MESSAGE - 1, PEERS, stride=MESSAGE), :]
    hits = jnp.concatenate(
        [jnp.where(meta[:, r : r + 1] == lane.astype(F32), 1.0, 0.0).T for r in range(SLOTS)], axis=1
    ).astype(BF16)
    ghost_layer = (LAYERS + 1) * other
    for k in range(MOMENTS):
        received = jnp.concatenate(
            [
                incoming[pl.ds(r * MOMENTS + k, PEERS, stride=MESSAGE), :]
                for r in range(SLOTS)
            ],
            axis=0,
        )
        high = received.astype(BF16)
        low = (received - high.astype(F32)).astype(BF16)
        summed = jnp.dot(
            hits, jnp.concatenate([high, low], axis=1), preferred_element_type=F32
        )
        cells[pl.ds(plane(k, ghost_layer) + 8, ROWS), :] = summed[:, :FACES] + summed[:, FACES:]

    def outer(i, carry):
        layer_step(interface, i)
        return carry

    lax.fori_loop(0, ROWS // BLOCK, outer, 0)
    whole.wait_send()
    rim.wait_send()


def on_device(
    moments, courant_azimuth, courant_radial, courant_axial, shear, owner, target, ami_weight
):
    shape = (MOMENTS, LAYERS, ROWS, FACES)
    field = (LAYERS * ROWS, FACES)
    dma = pltpu.SemaphoreType.DMA
    updated = pl.pallas_call(
        kernel,
        out_shape=jax.ShapeDtypeStruct(shape, F32),
        in_specs=[pl.BlockSpec(memory_space=pltpu.HBM)] * 8,
        out_specs=pl.BlockSpec(memory_space=pltpu.VMEM),
        scratch_shapes=[
            pltpu.VMEM((MOMENTS * (LAYERS + 2) * PLANE, FACES), F32),
            pltpu.VMEM(field, F32),
            pltpu.VMEM(field, F32),
            pltpu.VMEM(field, F32),
            pltpu.VMEM(field, F32),
            pltpu.VMEM((1, ROWS), jnp.int32),
            pltpu.VMEM((1, ROWS), jnp.int32),
            pltpu.VMEM((ROWS * FACES, FACES), F32),
            pltpu.VMEM((MOMENTS * ROWS, FACES), F32),
            pltpu.VMEM((ROWS + 1, 8, FACES), F32),
            pltpu.VMEM((8, PEERS), jnp.int32),
            pltpu.SMEM((8, PEERS), jnp.int32),
            pltpu.VMEM((MESSAGE * PEERS, FACES), F32),
            pltpu.VMEM((MESSAGE * PEERS, FACES), F32),
            pltpu.VMEM((ROWS, FACES), F32),
            pltpu.VMEM((ROWS, FACES), F32),
            dma((7,)),
            dma((MOMENTS + MOMENTS * LAYERS,)),
            dma((CHUNKS,)),
            dma,
            dma,
            dma,
            dma,
        ],
        compiler_params=pltpu.CompilerParams(
            collective_id=0, has_side_effects=True, vmem_limit_bytes=48 * 1024 * 1024
        ),
        name="transport",
    )(
        *[
            pltpu.with_memory_space_constraint(operand, pltpu.HBM)
            for operand in (
                moments.reshape(shape),
                courant_azimuth.reshape(field),
                courant_radial.reshape(field),
                courant_axial.reshape(field),
                shear.reshape(field),
                owner.reshape(1, ROWS),
                target.reshape(1, ROWS),
                ami_weight.reshape(ROWS * FACES, FACES),
            )
        ]
    )
    return updated[None]


def solution(mesh):
    placed = (
        P("region", None, None, None, "cells"),
        P("region", None, None, "cells"),
        P("region", None, None, "cells"),
        P("region", None, None, "cells"),
        P("region", None, None, "cells"),
        P("region", "cells", None),
        P("region", "cells"),
        P("region", "cells", None, None),
    )
    return jax.shard_map(
        on_device,
        mesh=mesh,
        in_specs=placed,
        out_specs=P("region", None, None, None, "cells"),
        check_vma=False,
    )
```

```python
import functools

import jax
import jax.numpy as jnp
from jax import lax
from jax.experimental import pallas as pl
from jax.experimental.pallas import tpu as pltpu
from jax.sharding import PartitionSpec as P

MESH = pl.DeviceIdType.MESH
F32 = jnp.float32
BF16 = jnp.bfloat16
KAGG = 0.005
KBRK = 0.02
LAYERS = 4
ROWS = 128
FACES = 128
MOMENTS = 6
PEERS = 128
SLOTS = 2
MESSAGE = SLOTS * MOMENTS
DEPTH = 8
FLAT = PEERS // DEPTH
PLANE = ROWS + 16
CHUNKS = 8
EARLY = 32
BLOCK = 32
CUBE_ROOT_2 = 2.0 ** (1.0 / 3.0)

THIRD_ANGLE = (
    0.5000000032577528,
    0.5773497198231888,
    -0.11109568329657703,
    0.053288656003267744,
    -0.03196129546407778,
    0.019675718215576045,
    -0.01032549308338918,
    0.003707686483927317,
    -0.0006393143691536856,
)


def third_angle(s):
    value = THIRD_ANGLE[-1] * s + THIRD_ANGLE[-2]
    for coefficient in THIRD_ANGLE[-3::-1]:
        value = value * s + coefficient
    return value


def quadrature(moment):
    mass = moment[0]
    inverse = 1.0 / mass
    n1, n2, n3, n4, n5 = [moment[degree] * inverse for degree in range(1, 6)]
    a0 = n1
    p1 = n2 - a0 * n1
    p2 = n3 - a0 * n2
    p3 = n4 - a0 * n3
    p4 = n5 - a0 * n4
    over_p1 = 1.0 / p1
    ratio = p2 * over_p1
    a1 = ratio - a0
    q2 = p3 - a1 * p2 - p1 * n2
    q3 = p4 - a1 * p3 - p1 * n3
    over_q2 = 1.0 / q2
    a2 = q3 * over_q2 - ratio
    b2 = q2 * over_p1
    centre = (a0 + a1 + a2) * (1.0 / 3.0)
    d0 = a0 - centre
    d1 = a1 - centre
    d2 = a2 - centre
    square = (d0 * d0 + d1 * d1 + d2 * d2 + 2.0 * (p1 + b2)) * (1.0 / 6.0)
    over_h = lax.rsqrt(square)
    h2 = 2.0 * square * over_h
    determ = d0 * (d1 * d2 - b2) - p1 * d2
    half_cosine = jnp.clip(0.25 * determ * (over_h * over_h * over_h), -0.5, 0.5)
    high = centre + h2 * third_angle(jnp.sqrt(0.5 + half_cosine))
    low = centre - h2 * third_angle(jnp.sqrt(0.5 - half_cosine))
    middle = 3.0 * centre - high - low
    nodes = [low, middle, high]
    weights = []
    for node in nodes:
        lead = node - a0
        trail = (node - a1) * lead - p1
        weights.append(mass / (1.0 + lead * lead * over_p1 + trail * trail * over_q2))
    return nodes, weights


def sources(moment, shear):
    nodes, weights = quadrature(moment)
    cubes = [node * node * node for node in nodes]
    merge = KAGG * shear
    split = KBRK * shear
    carried = [w * c for w, c in zip(weights, cubes)]
    born = [4.0 * w * a * merge for w, a in zip(weights, carried)]
    broken = [split * a for a in carried]
    lost = [2.0 * b + f for b, f in zip(born, broken)]
    terms, steps = [], []
    for first, second in ((0, 1), (0, 2), (1, 2)):
        summed = nodes[first] + nodes[second]
        pair = merge * (weights[first] * weights[second]) * (summed * summed * summed)
        lost[first] = lost[first] + pair
        lost[second] = lost[second] + pair
        terms.append(pair)
        steps.append(jnp.exp(jnp.log(cubes[first] + cubes[second]) * (1.0 / 3.0)))
    for index in range(3):
        terms += [born[index], 2.0 * broken[index], -lost[index]]
        node = nodes[index]
        steps += [CUBE_ROOT_2 * node, (1.0 / CUBE_ROOT_2) * node, node]
    result = []
    for degree in range(MOMENTS):
        if degree:
            terms = [term * step for term, step in zip(terms, steps)]
        total = moment[degree]
        for term in terms:
            total = total + term
        result.append(total)
    return result


def kernel(
    moments_hbm,
    azimuth_hbm,
    radial_hbm,
    axial_hbm,
    shear_hbm,
    owner_hbm,
    target_hbm,
    weight_hbm,
    out_ref,
    cells,
    azimuth,
    radial,
    axial,
    shear,
    owner,
    target,
    weight,
    face,
    contrib,
    index_vmem,
    index_smem,
    outgoing,
    incoming,
    rim_out,
    rim_in,
    rows_out,
    rows_in,
    partial,
    ghost_weight,
    small_sem,
    cell_sem,
    weight_sem,
    send_sem,
    recv_sem,
    rim_send_sem,
    rim_recv_sem,
    hop_send_sem,
    hop_recv_sem,
    rows_send_sem,
    rows_recv_sem,
):
    region = lax.axis_index("region")
    me = lax.axis_index("cells")
    other = 1 - region
    after = lax.rem(me + 1, PEERS)
    before = lax.rem(me + PEERS - 1, PEERS)
    interface = (LAYERS - 1) * other
    depth, flat = me // FLAT, lax.rem(me, FLAT)
    place = flat * DEPTH + depth
    per_chunk = ROWS // CHUNKS

    def plane(k, layer):
        return (k * (LAYERS + 2) + layer) * PLANE

    small = [
        pltpu.make_async_copy(owner_hbm, owner, small_sem.at[0]),
        pltpu.make_async_copy(target_hbm, target, small_sem.at[1]),
    ]
    for copy in small:
        copy.start()
    faces = [
        pltpu.make_async_copy(
            moments_hbm.at[k, interface], face.at[pl.ds(k * ROWS, ROWS)], cell_sem.at[k]
        )
        for k in range(MOMENTS)
    ]
    for copy in faces:
        copy.start()
    chunks = [
        pltpu.make_async_copy(
            weight_hbm.at[pl.ds(c * per_chunk * FACES, per_chunk * FACES)],
            weight.at[pl.ds(c * per_chunk * FACES, per_chunk * FACES)],
            weight_sem.at[c],
        )
        for c in range(CHUNKS)
    ]
    body_copies = []
    for k in range(MOMENTS):
        for layer in range(LAYERS):
            body_copies.append(
                pltpu.make_async_copy(
                    moments_hbm.at[k, layer],
                    cells.at[pl.ds(plane(k, layer + 1) + 8, ROWS)],
                    cell_sem.at[MOMENTS + k * LAYERS + layer],
                )
            )
    fields = [
        pltpu.make_async_copy(source, destination, small_sem.at[2 + i])
        for i, (source, destination) in enumerate(
            ((azimuth_hbm, azimuth), (radial_hbm, radial), (axial_hbm, axial), (shear_hbm, shear))
        )
    ]
    for copy in chunks + body_copies:
        copy.start()

    barrier = pltpu.get_barrier_semaphore()

    def greet(peer, carry):
        pl.semaphore_signal(barrier, inc=1, device_id=(other, peer), device_id_type=MESH)
        return carry

    lax.fori_loop(0, PEERS, greet, 0, unroll=8)
    column = [lax.rem(depth + i, DEPTH) * FLAT + flat for i in range(1, DEPTH)]
    near = [after, before] + column
    for peer in near:
        pl.semaphore_signal(barrier, inc=1, device_id=(region, peer), device_id_type=MESH)

    for copy in small:
        copy.wait()
    square = (ROWS, PEERS)
    sublane = lax.broadcasted_iota(jnp.int32, square, 0)
    lane = lax.broadcasted_iota(jnp.int32, square, 1)
    by_lane = jnp.broadcast_to(owner[...], square)
    by_sublane = by_lane.T
    same = by_lane == by_sublane
    rank = jnp.sum(jnp.where(same & (lane < sublane), 1, 0), axis=1, keepdims=True)
    target_column = jnp.broadcast_to(target[...], square).T
    index_vmem[...] = jnp.zeros(index_vmem.shape, jnp.int32)
    for r in range(SLOTS):
        chosen = (by_sublane == lane) & (rank == r)
        index = ROWS + jnp.sum(jnp.where(chosen, sublane - ROWS, 0), axis=0, keepdims=True)
        index_vmem[r : r + 1, :] = index
        row = jnp.sum(jnp.where(chosen, target_column, 0), axis=0, keepdims=True)
        rows_out[pl.ds(r * DEPTH + depth, 1), :] = row
    to_scalar = pltpu.make_async_copy(index_vmem, index_smem, small_sem.at[6])
    to_scalar.start()

    contrib[ROWS] = jnp.zeros((8, FACES), F32)
    for copy in faces:
        copy.wait()

    def weigh(z, carry):
        source = face[pl.ds(z, MOMENTS, stride=ROWS), :]
        source = jnp.concatenate([source, jnp.zeros((2, FACES), F32)], axis=0)
        source_high = source.astype(BF16).astype(F32)
        both = jnp.concatenate([source_high, source - source_high], axis=0).astype(BF16)
        matrix = weight[pl.ds(pl.multiple_of(z * FACES, FACES), FACES), :]
        high = matrix.astype(BF16)
        low = (matrix - high.astype(F32)).astype(BF16)
        product = lax.dot_general(
            both,
            jnp.concatenate([high, low], axis=0),
            (((1,), (1,)), ((), ())),
            preferred_element_type=F32,
        )
        contrib[z] = (
            product[:8, :FACES] + (product[8:, :FACES] + product[:8, FACES:])
        )
        return carry

    for c in range(CHUNKS):
        chunks[c].wait()
        lax.fori_loop(c * per_chunk, (c + 1) * per_chunk, weigh, 0, unroll=per_chunk)
    for copy in fields:
        copy.start()
    to_scalar.wait()

    pl.semaphore_wait(barrier, PEERS + len(near))

    for peer in column:
        for r in range(SLOTS):
            row = rows_out.at[pl.ds(r * DEPTH + depth, 1)]
            pltpu.make_async_remote_copy(
                src_ref=row,
                dst_ref=row,
                send_sem=hop_send_sem,
                recv_sem=hop_recv_sem,
                device_id=(region, peer),
                device_id_type=MESH,
            ).start()

    def dispatch(peer, carry):
        for r in range(SLOTS):
            block = index_smem[r, peer]
            values = contrib[block]
            outgoing[pl.ds(MESSAGE * peer + MOMENTS * r, MOMENTS), :] = values[:MOMENTS]
        pltpu.make_async_remote_copy(
            src_ref=outgoing.at[pl.ds(MESSAGE * peer, MESSAGE)],
            dst_ref=incoming.at[pl.ds(MESSAGE * place, MESSAGE)],
            send_sem=send_sem,
            recv_sem=recv_sem,
            device_id=(other, peer),
            device_id_type=MESH,
        ).start()
        return carry


    for copy in body_copies:
        copy.wait()
    lanes = lax.broadcasted_iota(jnp.int32, (8, FACES), 1)

    def pack(i, carry):
        packed = jnp.zeros((8, FACES), F32)
        for k in range(MOMENTS):
            for layer in range(LAYERS):
                p = k * LAYERS + layer
                values = cells[pl.ds(pl.multiple_of(plane(k, layer + 1) + 8 + i * 8, 8), 8), :]
                packed = jnp.where(lanes == p, pltpu.roll(values, p + 1, 1), packed)
        rim_out[pl.ds(pl.multiple_of(i * 8, 8), 8), :] = packed
        return carry

    lax.fori_loop(0, ROWS // 8, pack, 0)
    rim = pltpu.make_async_remote_copy(
        src_ref=rim_out,
        dst_ref=rim_in,
        send_sem=rim_send_sem,
        recv_sem=rim_recv_sem,
        device_id=(region, after),
        device_id_type=MESH,
    )
    rim.start()

    lax.fori_loop(0, PEERS, dispatch, 0, unroll=2)

    hop = pltpu.make_async_remote_copy(
        src_ref=rows_out.at[pl.ds(0, SLOTS * (DEPTH - 1))],
        dst_ref=rows_out.at[pl.ds(0, SLOTS * (DEPTH - 1))],
        send_sem=hop_send_sem,
        recv_sem=hop_recv_sem,
        device_id=(region, after),
        device_id_type=MESH,
    )
    hop.wait_recv()

    def spread(i, carry):
        for r in range(SLOTS):
            pltpu.make_async_remote_copy(
                src_ref=rows_out.at[pl.ds(r * DEPTH, DEPTH)],
                dst_ref=rows_in.at[pl.ds(r * PEERS + flat * DEPTH, DEPTH)],
                send_sem=rows_send_sem,
                recv_sem=rows_recv_sem,
                device_id=(other, depth * FLAT + i),
                device_id_type=MESH,
            ).start()
        return carry

    lax.fori_loop(0, FLAT, spread, 0)

    zero_rows = jnp.zeros((8, FACES), F32)

    def edges(i, carry):
        base = pl.multiple_of(i * PLANE, 8)
        cells[pl.ds(base, 8), :] = zero_rows
        cells[pl.ds(base + 8 + ROWS, 8), :] = zero_rows
        return carry

    lax.fori_loop(0, MOMENTS * (LAYERS + 2), edges, 0)
    for k in range(MOMENTS):
        empty = plane(k, (LAYERS + 1) * region)
        cells[pl.ds(empty + 8, ROWS), :] = jnp.zeros((ROWS, FACES), F32)

    for copy in fields:
        copy.wait()
    rim.wait_recv()
    lanes_block = lax.broadcasted_iota(jnp.int32, (BLOCK, FACES), 1)

    def advect(layer, i, at_interface):
        start = pl.multiple_of(i * BLOCK, BLOCK)
        at = pl.multiple_of(layer * ROWS + start, BLOCK)
        ca = azimuth[pl.ds(at, BLOCK), :]
        cr = radial[pl.ds(at, BLOCK), :]
        cz = axial[pl.ds(at, BLOCK), :]
        outward = cr > 0.0
        upward = cz > 0.0
        cr = jnp.abs(cr)
        cz = jnp.abs(cz)
        keep = 1.0 - ca - cr - cz
        rims = rim_in[pl.ds(start, BLOCK), :]
        if at_interface:
            from_ghost = outward == (region == 1)
            ghost_weight[pl.ds(start, BLOCK), :] = jnp.where(from_ghost, cr, 0.0)
            cr = jnp.where(from_ghost, 0.0, cr)
        advected = []
        for k in range(MOMENTS):
            row = plane(k, layer + 1) + 8 + start
            m = cells[pl.ds(row, BLOCK), :]
            shift = lax.rem(2 * FACES - (k * LAYERS + layer), FACES)
            previous = jnp.where(
                lanes_block == 0, pltpu.roll(rims, shift, 1), pltpu.roll(m, 1, 1)
            )
            axial_below = cells[pl.ds(row - 1, BLOCK), :]
            axial_beyond = cells[pl.ds(row + 1, BLOCK), :]
            if at_interface:
                radial_side = cells[pl.ds(row + (2 * region - 1) * PLANE, BLOCK), :]
            else:
                below = cells[pl.ds(row - PLANE, BLOCK), :]
                beyond = cells[pl.ds(row + PLANE, BLOCK), :]
                radial_side = jnp.where(outward, below, beyond)
            advected.append(
                keep * m
                + ca * previous
                + cr * radial_side
                + cz * jnp.where(upward, axial_below, axial_beyond)
            )
        return advected

    def finish(layer, i, advected):
        start = pl.multiple_of(i * BLOCK, BLOCK)
        at = pl.multiple_of(layer * ROWS + start, BLOCK)
        result = sources(advected, shear[pl.ds(at, BLOCK), :])
        for k in range(MOMENTS):
            out_ref[k, layer, pl.ds(start, BLOCK), :] = result[k]

    def inner(n, carry):
        layer = region + n // (ROWS // BLOCK)
        i = lax.rem(n, ROWS // BLOCK)
        finish(layer, i, advect(layer, i, False))
        return carry

    lax.fori_loop(0, (LAYERS - 1) * (ROWS // BLOCK), inner, 0)

    def prepare(i, carry):
        advected = advect(interface, i, True)
        for k in range(MOMENTS):
            partial[pl.ds(pl.multiple_of(k * ROWS + i * BLOCK, BLOCK), BLOCK), :] = advected[k]
        return carry

    lax.fori_loop(0, ROWS // BLOCK, prepare, 0)

    rows = pltpu.make_async_remote_copy(
        src_ref=rows_in,
        dst_ref=rows_in,
        send_sem=rows_send_sem,
        recv_sem=rows_recv_sem,
        device_id=(other, me),
        device_id_type=MESH,
    )
    rows.wait_recv()
    mine = []
    for r in range(SLOTS):
        named = jnp.where(lane == me, rows_in[pl.ds(r * PEERS, PEERS), :], 0)
        named = jnp.sum(named, axis=1, keepdims=True)
        mine.append(jnp.where(named == lane, 1.0, 0.0).T)
    hits = jnp.concatenate(mine, axis=1).astype(BF16)

    whole = pltpu.make_async_remote_copy(
        src_ref=outgoing,
        dst_ref=incoming,
        send_sem=send_sem,
        recv_sem=recv_sem,
        device_id=(other, me),
        device_id_type=MESH,
    )
    whole.wait_recv()

    for k in range(MOMENTS):
        received = jnp.concatenate(
            [
                incoming[pl.ds(r * MOMENTS + k, PEERS, stride=MESSAGE), :]
                for r in range(SLOTS)
            ],
            axis=0,
        )
        high = received.astype(BF16)
        low = (received - high.astype(F32)).astype(BF16)
        summed = jnp.dot(
            hits, jnp.concatenate([high, low], axis=1), preferred_element_type=F32
        )
        ghost = summed[:, :FACES] + summed[:, FACES:]
        at = pl.ds(k * ROWS, ROWS)
        partial[at, :] = partial[at, :] + ghost_weight[...] * ghost

    def outer(i, carry):
        advected = [
            partial[pl.ds(pl.multiple_of(k * ROWS + i * BLOCK, BLOCK), BLOCK), :]
            for k in range(MOMENTS)
        ]
        finish(interface, i, advected)
        return carry

    lax.fori_loop(0, ROWS // BLOCK, outer, 0)
    whole.wait_send()
    rim.wait_send()
    hop.wait_send()
    rows.wait_send()


def on_device(
    moments, courant_azimuth, courant_radial, courant_axial, shear, owner, target, ami_weight
):
    shape = (MOMENTS, LAYERS, ROWS, FACES)
    field = (LAYERS * ROWS, FACES)
    dma = pltpu.SemaphoreType.DMA
    updated = pl.pallas_call(
        kernel,
        out_shape=jax.ShapeDtypeStruct(shape, F32),
        in_specs=[pl.BlockSpec(memory_space=pltpu.HBM)] * 8,
        out_specs=pl.BlockSpec(memory_space=pltpu.VMEM),
        scratch_shapes=[
            pltpu.VMEM((MOMENTS * (LAYERS + 2) * PLANE, FACES), F32),
            pltpu.VMEM(field, F32),
            pltpu.VMEM(field, F32),
            pltpu.VMEM(field, F32),
            pltpu.VMEM(field, F32),
            pltpu.VMEM((1, ROWS), jnp.int32),
            pltpu.VMEM((1, ROWS), jnp.int32),
            pltpu.VMEM((ROWS * FACES, FACES), F32),
            pltpu.VMEM((MOMENTS * ROWS, FACES), F32),
            pltpu.VMEM((ROWS + 1, 8, FACES), F32),
            pltpu.VMEM((8, PEERS), jnp.int32),
            pltpu.SMEM((8, PEERS), jnp.int32),
            pltpu.VMEM((MESSAGE * PEERS, FACES), F32),
            pltpu.VMEM((MESSAGE * PEERS, FACES), F32),
            pltpu.VMEM((ROWS, FACES), F32),
            pltpu.VMEM((ROWS, FACES), F32),
            pltpu.VMEM((SLOTS * DEPTH, PEERS), jnp.int32),
            pltpu.VMEM((SLOTS * PEERS, PEERS), jnp.int32),
            pltpu.VMEM((MOMENTS * ROWS, FACES), F32),
            pltpu.VMEM((ROWS, FACES), F32),
            dma((7,)),
            dma((MOMENTS + MOMENTS * LAYERS,)),
            dma((CHUNKS,)),
            dma,
            dma,
            dma,
            dma,
            dma,
            dma,
            dma,
            dma,
        ],
        compiler_params=pltpu.CompilerParams(
            collective_id=0, has_side_effects=True, vmem_limit_bytes=48 * 1024 * 1024
        ),
        name="transport",
    )(
        *[
            pltpu.with_memory_space_constraint(operand, pltpu.HBM)
            for operand in (
                moments.reshape(shape),
                courant_azimuth.reshape(field),
                courant_radial.reshape(field),
                courant_axial.reshape(field),
                shear.reshape(field),
                owner.reshape(1, ROWS),
                target.reshape(1, ROWS),
                ami_weight.reshape(ROWS * FACES, FACES),
            )
        ]
    )
    return updated[None]


def solution(mesh):
    placed = (
        P("region", None, None, None, "cells"),
        P("region", None, None, "cells"),
        P("region", None, None, "cells"),
        P("region", None, None, "cells"),
        P("region", None, None, "cells"),
        P("region", "cells", None),
        P("region", "cells"),
        P("region", "cells", None, None),
    )
    return jax.shard_map(
        on_device,
        mesh=mesh,
        in_specs=placed,
        out_specs=P("region", None, None, None, "cells"),
        check_vma=False,
    )
```

```python
import functools

import jax
import jax.numpy as jnp
from jax import lax
from jax.experimental import pallas as pl
from jax.experimental.pallas import tpu as pltpu
from jax.sharding import PartitionSpec as P

MESH = pl.DeviceIdType.MESH
F32 = jnp.float32
BF16 = jnp.bfloat16
KAGG = 0.005
KBRK = 0.02
LAYERS = 4
ROWS = 128
FACES = 128
MOMENTS = 6
PEERS = 128
SLOTS = 2
MESSAGE = SLOTS * MOMENTS
DEPTH = 8
FLAT = PEERS // DEPTH
PLANE = ROWS + 16
CHUNKS = 8
EARLY = 32
BLOCK = 32
CUBE_ROOT_2 = 2.0 ** (1.0 / 3.0)

THIRD_ANGLE = (
    0.5000000032577528,
    0.5773497198231888,
    -0.11109568329657703,
    0.053288656003267744,
    -0.03196129546407778,
    0.019675718215576045,
    -0.01032549308338918,
    0.003707686483927317,
    -0.0006393143691536856,
)


def third_angle(s):
    value = THIRD_ANGLE[-1] * s + THIRD_ANGLE[-2]
    for coefficient in THIRD_ANGLE[-3::-1]:
        value = value * s + coefficient
    return value


def quadrature(moment):
    mass = moment[0]
    inverse = 1.0 / mass
    n1, n2, n3, n4, n5 = [moment[degree] * inverse for degree in range(1, 6)]
    a0 = n1
    p1 = n2 - a0 * n1
    p2 = n3 - a0 * n2
    p3 = n4 - a0 * n3
    p4 = n5 - a0 * n4
    over_p1 = 1.0 / p1
    ratio = p2 * over_p1
    a1 = ratio - a0
    q2 = p3 - a1 * p2 - p1 * n2
    q3 = p4 - a1 * p3 - p1 * n3
    over_q2 = 1.0 / q2
    a2 = q3 * over_q2 - ratio
    b2 = q2 * over_p1
    centre = (a0 + a1 + a2) * (1.0 / 3.0)
    d0 = a0 - centre
    d1 = a1 - centre
    d2 = a2 - centre
    square = (d0 * d0 + d1 * d1 + d2 * d2 + 2.0 * (p1 + b2)) * (1.0 / 6.0)
    over_h = lax.rsqrt(square)
    h2 = 2.0 * square * over_h
    determ = d0 * (d1 * d2 - b2) - p1 * d2
    half_cosine = jnp.clip(0.25 * determ * (over_h * over_h * over_h), -0.5, 0.5)
    high = centre + h2 * third_angle(jnp.sqrt(0.5 + half_cosine))
    low = centre - h2 * third_angle(jnp.sqrt(0.5 - half_cosine))
    middle = 3.0 * centre - high - low
    nodes = [low, middle, high]
    weights = []
    for node in nodes:
        lead = node - a0
        trail = (node - a1) * lead - p1
        weights.append(mass / (1.0 + lead * lead * over_p1 + trail * trail * over_q2))
    return nodes, weights


def sources(moment, shear):
    nodes, weights = quadrature(moment)
    cubes = [node * node * node for node in nodes]
    merge = KAGG * shear
    split = KBRK * shear
    carried = [w * c for w, c in zip(weights, cubes)]
    born = [4.0 * w * a * merge for w, a in zip(weights, carried)]
    broken = [split * a for a in carried]
    lost = [2.0 * b + f for b, f in zip(born, broken)]
    terms, steps = [], []
    for first, second in ((0, 1), (0, 2), (1, 2)):
        summed = nodes[first] + nodes[second]
        pair = merge * (weights[first] * weights[second]) * (summed * summed * summed)
        lost[first] = lost[first] + pair
        lost[second] = lost[second] + pair
        terms.append(pair)
        steps.append(jnp.exp(jnp.log(cubes[first] + cubes[second]) * (1.0 / 3.0)))
    for index in range(3):
        terms += [born[index], 2.0 * broken[index], -lost[index]]
        node = nodes[index]
        steps += [CUBE_ROOT_2 * node, (1.0 / CUBE_ROOT_2) * node, node]
    result = []
    for degree in range(MOMENTS):
        if degree:
            terms = [term * step for term, step in zip(terms, steps)]
        total = moment[degree]
        for term in terms:
            total = total + term
        result.append(total)
    return result


def kernel(
    moments_hbm,
    azimuth_hbm,
    radial_hbm,
    axial_hbm,
    shear_hbm,
    owner_hbm,
    target_hbm,
    weight_hbm,
    out_ref,
    cells,
    azimuth,
    radial,
    axial,
    shear,
    owner,
    target,
    weight,
    face,
    contrib,
    index_vmem,
    index_smem,
    outgoing,
    incoming,
    rim_out,
    rim_in,
    rows_out,
    rows_in,
    partial,
    ghost_weight,
    small_sem,
    cell_sem,
    weight_sem,
    send_sem,
    recv_sem,
    rim_send_sem,
    rim_recv_sem,
    hop_send_sem,
    hop_recv_sem,
    rows_send_sem,
    rows_recv_sem,
):
    region = lax.axis_index("region")
    me = lax.axis_index("cells")
    other = 1 - region
    after = lax.rem(me + 1, PEERS)
    before = lax.rem(me + PEERS - 1, PEERS)
    interface = (LAYERS - 1) * other
    depth, flat = me // FLAT, lax.rem(me, FLAT)
    place = flat * DEPTH + depth
    per_chunk = ROWS // CHUNKS

    def plane(k, layer):
        return (k * (LAYERS + 2) + layer) * PLANE

    small = [
        pltpu.make_async_copy(owner_hbm, owner, small_sem.at[0]),
        pltpu.make_async_copy(target_hbm, target, small_sem.at[1]),
    ]
    for copy in small:
        copy.start()
    faces = [
        pltpu.make_async_copy(
            moments_hbm.at[k, interface], face.at[pl.ds(k * ROWS, ROWS)], cell_sem.at[k]
        )
        for k in range(MOMENTS)
    ]
    for copy in faces:
        copy.start()
    chunks = [
        pltpu.make_async_copy(
            weight_hbm.at[pl.ds(c * per_chunk * FACES, per_chunk * FACES)],
            weight.at[pl.ds(c * per_chunk * FACES, per_chunk * FACES)],
            weight_sem.at[c],
        )
        for c in range(CHUNKS)
    ]
    body_copies = []
    for k in range(MOMENTS):
        for layer in range(LAYERS):
            body_copies.append(
                pltpu.make_async_copy(
                    moments_hbm.at[k, layer],
                    cells.at[pl.ds(plane(k, layer + 1) + 8, ROWS)],
                    cell_sem.at[MOMENTS + k * LAYERS + layer],
                )
            )
    fields = [
        pltpu.make_async_copy(source, destination, small_sem.at[2 + i])
        for i, (source, destination) in enumerate(
            ((azimuth_hbm, azimuth), (radial_hbm, radial), (axial_hbm, axial), (shear_hbm, shear))
        )
    ]
    for copy in chunks + body_copies + fields:
        copy.start()

    barrier = pltpu.get_barrier_semaphore()

    def greet(peer, carry):
        pl.semaphore_signal(barrier, inc=1, device_id=(other, peer), device_id_type=MESH)
        return carry

    lax.fori_loop(0, PEERS, greet, 0, unroll=8)
    column = [lax.rem(depth + i, DEPTH) * FLAT + flat for i in range(1, DEPTH)]
    near = [after, before] + column
    for peer in near:
        pl.semaphore_signal(barrier, inc=1, device_id=(region, peer), device_id_type=MESH)

    for copy in small:
        copy.wait()
    square = (ROWS, PEERS)
    sublane = lax.broadcasted_iota(jnp.int32, square, 0)
    lane = lax.broadcasted_iota(jnp.int32, square, 1)
    by_lane = jnp.broadcast_to(owner[...], square)
    by_sublane = by_lane.T
    same = by_lane == by_sublane
    rank = jnp.sum(jnp.where(same & (lane < sublane), 1, 0), axis=1, keepdims=True)
    target_column = jnp.broadcast_to(target[...], square).T
    index_vmem[...] = jnp.zeros(index_vmem.shape, jnp.int32)
    for r in range(SLOTS):
        chosen = (by_sublane == lane) & (rank == r)
        index = ROWS + jnp.sum(jnp.where(chosen, sublane - ROWS, 0), axis=0, keepdims=True)
        index_vmem[r : r + 1, :] = index
        row = jnp.sum(jnp.where(chosen, target_column, 0), axis=0, keepdims=True)
        rows_out[pl.ds(r * DEPTH + depth, 1), :] = row
    to_scalar = pltpu.make_async_copy(index_vmem, index_smem, small_sem.at[6])
    to_scalar.start()

    contrib[ROWS] = jnp.zeros((8, FACES), F32)
    for copy in faces:
        copy.wait()

    def weigh(z, carry):
        source = face[pl.ds(z, MOMENTS, stride=ROWS), :]
        source = jnp.concatenate([source, jnp.zeros((2, FACES), F32)], axis=0)
        source_high = source.astype(BF16).astype(F32)
        both = jnp.concatenate([source_high, source - source_high], axis=0).astype(BF16)
        matrix = weight[pl.ds(pl.multiple_of(z * FACES, FACES), FACES), :]
        high = matrix.astype(BF16)
        low = (matrix - high.astype(F32)).astype(BF16)
        product = lax.dot_general(
            both,
            jnp.concatenate([high, low], axis=0),
            (((1,), (1,)), ((), ())),
            preferred_element_type=F32,
        )
        contrib[z] = (
            product[:8, :FACES] + (product[8:, :FACES] + product[:8, FACES:])
        )
        return carry

    for c in range(CHUNKS):
        chunks[c].wait()
        lax.fori_loop(c * per_chunk, (c + 1) * per_chunk, weigh, 0, unroll=per_chunk)
    to_scalar.wait()

    pl.semaphore_wait(barrier, PEERS + len(near))

    for peer in column:
        for r in range(SLOTS):
            row = rows_out.at[pl.ds(r * DEPTH + depth, 1)]
            pltpu.make_async_remote_copy(
                src_ref=row,
                dst_ref=row,
                send_sem=hop_send_sem,
                recv_sem=hop_recv_sem,
                device_id=(region, peer),
                device_id_type=MESH,
            ).start()

    def dispatch(peer, carry):
        for r in range(SLOTS):
            block = index_smem[r, peer]
            values = contrib[block]
            outgoing[pl.ds(MESSAGE * peer + MOMENTS * r, MOMENTS), :] = values[:MOMENTS]
        pltpu.make_async_remote_copy(
            src_ref=outgoing.at[pl.ds(MESSAGE * peer, MESSAGE)],
            dst_ref=incoming.at[pl.ds(MESSAGE * place, MESSAGE)],
            send_sem=send_sem,
            recv_sem=recv_sem,
            device_id=(other, peer),
            device_id_type=MESH,
        ).start()
        return carry


    for copy in body_copies:
        copy.wait()
    lanes = lax.broadcasted_iota(jnp.int32, (8, FACES), 1)

    def pack(i, carry):
        packed = jnp.zeros((8, FACES), F32)
        for k in range(MOMENTS):
            for layer in range(LAYERS):
                p = k * LAYERS + layer
                values = cells[pl.ds(pl.multiple_of(plane(k, layer + 1) + 8 + i * 8, 8), 8), :]
                packed = jnp.where(lanes == p, pltpu.roll(values, p + 1, 1), packed)
        rim_out[pl.ds(pl.multiple_of(i * 8, 8), 8), :] = packed
        return carry

    lax.fori_loop(0, ROWS // 8, pack, 0, unroll=4)
    rim = pltpu.make_async_remote_copy(
        src_ref=rim_out,
        dst_ref=rim_in,
        send_sem=rim_send_sem,
        recv_sem=rim_recv_sem,
        device_id=(region, after),
        device_id_type=MESH,
    )
    rim.start()

    lax.fori_loop(0, PEERS, dispatch, 0, unroll=2)

    hop = pltpu.make_async_remote_copy(
        src_ref=rows_out.at[pl.ds(0, SLOTS * (DEPTH - 1))],
        dst_ref=rows_out.at[pl.ds(0, SLOTS * (DEPTH - 1))],
        send_sem=hop_send_sem,
        recv_sem=hop_recv_sem,
        device_id=(region, after),
        device_id_type=MESH,
    )
    hop.wait_recv()

    def spread(i, carry):
        for r in range(SLOTS):
            pltpu.make_async_remote_copy(
                src_ref=rows_out.at[pl.ds(r * DEPTH, DEPTH)],
                dst_ref=rows_in.at[pl.ds(r * PEERS + flat * DEPTH, DEPTH)],
                send_sem=rows_send_sem,
                recv_sem=rows_recv_sem,
                device_id=(other, depth * FLAT + i),
                device_id_type=MESH,
            ).start()
        return carry

    lax.fori_loop(0, FLAT, spread, 0)

    zero_rows = jnp.zeros((8, FACES), F32)

    def edges(i, carry):
        base = pl.multiple_of(i * PLANE, 8)
        cells[pl.ds(base, 8), :] = zero_rows
        cells[pl.ds(base + 8 + ROWS, 8), :] = zero_rows
        return carry

    lax.fori_loop(0, MOMENTS * (LAYERS + 2), edges, 0)
    for k in range(MOMENTS):
        empty = plane(k, (LAYERS + 1) * region)
        cells[pl.ds(empty + 8, ROWS), :] = jnp.zeros((ROWS, FACES), F32)

    for copy in fields:
        copy.wait()
    rim.wait_recv()
    lanes_block = lax.broadcasted_iota(jnp.int32, (BLOCK, FACES), 1)

    def advect(layer, i, at_interface):
        start = pl.multiple_of(i * BLOCK, BLOCK)
        at = pl.multiple_of(layer * ROWS + start, BLOCK)
        ca = azimuth[pl.ds(at, BLOCK), :]
        cr = radial[pl.ds(at, BLOCK), :]
        cz = axial[pl.ds(at, BLOCK), :]
        outward = cr > 0.0
        upward = cz > 0.0
        cr = jnp.abs(cr)
        cz = jnp.abs(cz)
        keep = 1.0 - ca - cr - cz
        rims = rim_in[pl.ds(start, BLOCK), :]
        if at_interface:
            from_ghost = outward == (region == 1)
            ghost_weight[pl.ds(start, BLOCK), :] = jnp.where(from_ghost, cr, 0.0)
            cr = jnp.where(from_ghost, 0.0, cr)
        advected = []
        for k in range(MOMENTS):
            row = plane(k, layer + 1) + 8 + start
            m = cells[pl.ds(row, BLOCK), :]
            shift = lax.rem(2 * FACES - (k * LAYERS + layer), FACES)
            previous = jnp.where(
                lanes_block == 0, pltpu.roll(rims, shift, 1), pltpu.roll(m, 1, 1)
            )
            axial_below = cells[pl.ds(row - 1, BLOCK), :]
            axial_beyond = cells[pl.ds(row + 1, BLOCK), :]
            if at_interface:
                radial_side = cells[pl.ds(row + (2 * region - 1) * PLANE, BLOCK), :]
            else:
                below = cells[pl.ds(row - PLANE, BLOCK), :]
                beyond = cells[pl.ds(row + PLANE, BLOCK), :]
                radial_side = jnp.where(outward, below, beyond)
            advected.append(
                keep * m
                + ca * previous
                + cr * radial_side
                + cz * jnp.where(upward, axial_below, axial_beyond)
            )
        return advected

    def finish(layer, i, advected):
        start = pl.multiple_of(i * BLOCK, BLOCK)
        at = pl.multiple_of(layer * ROWS + start, BLOCK)
        result = sources(advected, shear[pl.ds(at, BLOCK), :])
        for k in range(MOMENTS):
            out_ref[k, layer, pl.ds(start, BLOCK), :] = result[k]

    def inner(n, carry):
        layer = region + n // (ROWS // BLOCK)
        i = lax.rem(n, ROWS // BLOCK)
        finish(layer, i, advect(layer, i, False))
        return carry

    lax.fori_loop(0, (LAYERS - 1) * (ROWS // BLOCK), inner, 0)

    def prepare(i, carry):
        advected = advect(interface, i, True)
        for k in range(MOMENTS):
            partial[pl.ds(pl.multiple_of(k * ROWS + i * BLOCK, BLOCK), BLOCK), :] = advected[k]
        return carry

    lax.fori_loop(0, ROWS // BLOCK, prepare, 0)

    rows = pltpu.make_async_remote_copy(
        src_ref=rows_in,
        dst_ref=rows_in,
        send_sem=rows_send_sem,
        recv_sem=rows_recv_sem,
        device_id=(other, me),
        device_id_type=MESH,
    )
    rows.wait_recv()
    mine = []
    for r in range(SLOTS):
        named = jnp.where(lane == me, rows_in[pl.ds(r * PEERS, PEERS), :], 0)
        named = jnp.sum(named, axis=1, keepdims=True)
        mine.append(jnp.where(named == lane, 1.0, 0.0).T)
    hits = jnp.concatenate(mine, axis=1).astype(BF16)

    whole = pltpu.make_async_remote_copy(
        src_ref=outgoing,
        dst_ref=incoming,
        send_sem=send_sem,
        recv_sem=recv_sem,
        device_id=(other, me),
        device_id_type=MESH,
    )
    whole.wait_recv()

    for k in range(MOMENTS):
        received = jnp.concatenate(
            [
                incoming[pl.ds(r * MOMENTS + k, PEERS, stride=MESSAGE), :]
                for r in range(SLOTS)
            ],
            axis=0,
        )
        high = received.astype(BF16)
        low = (received - high.astype(F32)).astype(BF16)
        summed = jnp.dot(
            hits, jnp.concatenate([high, low], axis=1), preferred_element_type=F32
        )
        ghost = summed[:, :FACES] + summed[:, FACES:]
        at = pl.ds(k * ROWS, ROWS)
        partial[at, :] = partial[at, :] + ghost_weight[...] * ghost

    def outer(i, carry):
        advected = [
            partial[pl.ds(pl.multiple_of(k * ROWS + i * BLOCK, BLOCK), BLOCK), :]
            for k in range(MOMENTS)
        ]
        finish(interface, i, advected)
        return carry

    lax.fori_loop(0, ROWS // BLOCK, outer, 0)
    whole.wait_send()
    rim.wait_send()
    hop.wait_send()
    rows.wait_send()


def on_device(
    moments, courant_azimuth, courant_radial, courant_axial, shear, owner, target, ami_weight
):
    shape = (MOMENTS, LAYERS, ROWS, FACES)
    field = (LAYERS * ROWS, FACES)
    dma = pltpu.SemaphoreType.DMA
    updated = pl.pallas_call(
        kernel,
        out_shape=jax.ShapeDtypeStruct(shape, F32),
        in_specs=[pl.BlockSpec(memory_space=pltpu.HBM)] * 8,
        out_specs=pl.BlockSpec(memory_space=pltpu.VMEM),
        scratch_shapes=[
            pltpu.VMEM((MOMENTS * (LAYERS + 2) * PLANE, FACES), F32),
            pltpu.VMEM(field, F32),
            pltpu.VMEM(field, F32),
            pltpu.VMEM(field, F32),
            pltpu.VMEM(field, F32),
            pltpu.VMEM((1, ROWS), jnp.int32),
            pltpu.VMEM((1, ROWS), jnp.int32),
            pltpu.VMEM((ROWS * FACES, FACES), F32),
            pltpu.VMEM((MOMENTS * ROWS, FACES), F32),
            pltpu.VMEM((ROWS + 1, 8, FACES), F32),
            pltpu.VMEM((8, PEERS), jnp.int32),
            pltpu.SMEM((8, PEERS), jnp.int32),
            pltpu.VMEM((MESSAGE * PEERS, FACES), F32),
            pltpu.VMEM((MESSAGE * PEERS, FACES), F32),
            pltpu.VMEM((ROWS, FACES), F32),
            pltpu.VMEM((ROWS, FACES), F32),
            pltpu.VMEM((SLOTS * DEPTH, PEERS), jnp.int32),
            pltpu.VMEM((SLOTS * PEERS, PEERS), jnp.int32),
            pltpu.VMEM((MOMENTS * ROWS, FACES), F32),
            pltpu.VMEM((ROWS, FACES), F32),
            dma((7,)),
            dma((MOMENTS + MOMENTS * LAYERS,)),
            dma((CHUNKS,)),
            dma,
            dma,
            dma,
            dma,
            dma,
            dma,
            dma,
            dma,
        ],
        compiler_params=pltpu.CompilerParams(
            collective_id=0, has_side_effects=True, vmem_limit_bytes=48 * 1024 * 1024
        ),
        name="transport",
    )(
        *[
            pltpu.with_memory_space_constraint(operand, pltpu.HBM)
            for operand in (
                moments.reshape(shape),
                courant_azimuth.reshape(field),
                courant_radial.reshape(field),
                courant_axial.reshape(field),
                shear.reshape(field),
                owner.reshape(1, ROWS),
                target.reshape(1, ROWS),
                ami_weight.reshape(ROWS * FACES, FACES),
            )
        ]
    )
    return updated[None]


def solution(mesh):
    placed = (
        P("region", None, None, None, "cells"),
        P("region", None, None, "cells"),
        P("region", None, None, "cells"),
        P("region", None, None, "cells"),
        P("region", None, None, "cells"),
        P("region", "cells", None),
        P("region", "cells"),
        P("region", "cells", None, None),
    )
    return jax.shard_map(
        on_device,
        mesh=mesh,
        in_specs=placed,
        out_specs=P("region", None, None, None, "cells"),
        check_vma=False,
    )
```

```python
import functools

import jax
import jax.numpy as jnp
from jax import lax
from jax.experimental import pallas as pl
from jax.experimental.pallas import tpu as pltpu
from jax.sharding import PartitionSpec as P

MESH = pl.DeviceIdType.MESH
F32 = jnp.float32
BF16 = jnp.bfloat16
KAGG = 0.005
KBRK = 0.02
LAYERS = 4
ROWS = 128
FACES = 128
MOMENTS = 6
PEERS = 128
SLOTS = 2
PLANES = MOMENTS * LAYERS
MESSAGE = SLOTS * MOMENTS
DEPTH = 8
FLAT = PEERS // DEPTH
CHUNKS = 4
EARLY = 32
BLOCK = 32
CUBE_ROOT_2 = 2.0 ** (1.0 / 3.0)

THIRD_ANGLE = (
    0.5000000032577528,
    0.5773497198231888,
    -0.11109568329657703,
    0.053288656003267744,
    -0.03196129546407778,
    0.019675718215576045,
    -0.01032549308338918,
    0.003707686483927317,
    -0.0006393143691536856,
)


def third_angle(s):
    value = THIRD_ANGLE[-1] * s + THIRD_ANGLE[-2]
    for coefficient in THIRD_ANGLE[-3::-1]:
        value = value * s + coefficient
    return value


def quadrature(moment):
    mass = moment[0]
    inverse = 1.0 / mass
    n1, n2, n3, n4, n5 = [moment[degree] * inverse for degree in range(1, 6)]
    a0 = n1
    p1 = n2 - a0 * n1
    p2 = n3 - a0 * n2
    p3 = n4 - a0 * n3
    p4 = n5 - a0 * n4
    over_p1 = 1.0 / p1
    ratio = p2 * over_p1
    a1 = ratio - a0
    q2 = p3 - a1 * p2 - p1 * n2
    q3 = p4 - a1 * p3 - p1 * n3
    over_q2 = 1.0 / q2
    a2 = q3 * over_q2 - ratio
    b2 = q2 * over_p1
    centre = (a0 + a1 + a2) * (1.0 / 3.0)
    d0 = a0 - centre
    d1 = a1 - centre
    d2 = a2 - centre
    square = (d0 * d0 + d1 * d1 + d2 * d2 + 2.0 * (p1 + b2)) * (1.0 / 6.0)
    over_h = lax.rsqrt(square)
    h2 = 2.0 * square * over_h
    determ = d0 * (d1 * d2 - b2) - p1 * d2
    half_cosine = jnp.clip(0.25 * determ * (over_h * over_h * over_h), -0.5, 0.5)
    high = centre + h2 * third_angle(jnp.sqrt(0.5 + half_cosine))
    low = centre - h2 * third_angle(jnp.sqrt(0.5 - half_cosine))
    middle = 3.0 * centre - high - low
    nodes = [low, middle, high]
    weights = []
    for node in nodes:
        lead = node - a0
        trail = (node - a1) * lead - p1
        weights.append(mass / (1.0 + lead * lead * over_p1 + trail * trail * over_q2))
    return nodes, weights


def sources(moment, shear):
    nodes, weights = quadrature(moment)
    cubes = [node * node * node for node in nodes]
    merge = KAGG * shear
    split = KBRK * shear
    carried = [w * c for w, c in zip(weights, cubes)]
    born = [4.0 * w * a * merge for w, a in zip(weights, carried)]
    broken = [split * a for a in carried]
    lost = [2.0 * b + f for b, f in zip(born, broken)]
    terms, steps = [], []
    for first, second in ((0, 1), (0, 2), (1, 2)):
        summed = nodes[first] + nodes[second]
        pair = merge * (weights[first] * weights[second]) * (summed * summed * summed)
        lost[first] = lost[first] + pair
        lost[second] = lost[second] + pair
        terms.append(pair)
        steps.append(jnp.exp(jnp.log(cubes[first] + cubes[second]) * (1.0 / 3.0)))
    for index in range(3):
        terms += [born[index], 2.0 * broken[index], -lost[index]]
        node = nodes[index]
        steps += [CUBE_ROOT_2 * node, (1.0 / CUBE_ROOT_2) * node, node]
    result = []
    for degree in range(MOMENTS):
        if degree:
            terms = [term * step for term, step in zip(terms, steps)]
        total = moment[degree]
        for term in terms:
            total = total + term
        result.append(total)
    return result


def kernel(
    moments_hbm,
    azimuth_hbm,
    radial_hbm,
    axial_hbm,
    shear_hbm,
    owner_hbm,
    target_hbm,
    weight_hbm,
    out_ref,
    cells,
    azimuth,
    radial,
    axial,
    shear,
    owner,
    target,
    weight,
    face,
    contrib,
    index_vmem,
    index_smem,
    outgoing,
    incoming,
    rim_columns,
    rim_out,
    rim_in,
    rows_out,
    rows_in,
    partial,
    ghost_weight,
    small_sem,
    cell_sem,
    weight_sem,
    send_sem,
    recv_sem,
    rim_send_sem,
    rim_recv_sem,
    hop_send_sem,
    hop_recv_sem,
    rows_send_sem,
    rows_recv_sem,
):
    region = lax.axis_index("region")
    me = lax.axis_index("cells")
    other = 1 - region
    after = lax.rem(me + 1, PEERS)
    before = lax.rem(me + PEERS - 1, PEERS)
    interface = (LAYERS - 1) * other
    depth, flat = me // FLAT, lax.rem(me, FLAT)
    place = flat * DEPTH + depth
    per_chunk = ROWS // CHUNKS

    def plane(k, layer):
        return (k * (LAYERS + 2) + layer) * ROWS

    small = [
        pltpu.make_async_copy(owner_hbm, owner, small_sem.at[0]),
        pltpu.make_async_copy(target_hbm, target, small_sem.at[1]),
    ]
    for copy in small:
        copy.start()
    faces = [
        pltpu.make_async_copy(
            moments_hbm.at[k, pl.ds(pl.multiple_of(interface * ROWS, ROWS), ROWS)], face.at[pl.ds(k * ROWS, ROWS)], cell_sem.at[k]
        )
        for k in range(MOMENTS)
    ]
    for copy in faces:
        copy.start()
    chunks = [
        pltpu.make_async_copy(
            weight_hbm.at[pl.ds(c * per_chunk * FACES, per_chunk * FACES)],
            weight.at[pl.ds(c * per_chunk * FACES, per_chunk * FACES)],
            weight_sem.at[c],
        )
        for c in range(CHUNKS)
    ]
    body_copies = []
    for k in range(MOMENTS):
        body_copies.append(
            pltpu.make_async_copy(
                moments_hbm.at[k],
                cells.at[pl.ds(plane(k, 1), LAYERS * ROWS)],
                cell_sem.at[MOMENTS + k],
            )
        )
    fields = [
        pltpu.make_async_copy(source, destination, small_sem.at[2 + i])
        for i, (source, destination) in enumerate(
            ((azimuth_hbm, azimuth), (radial_hbm, radial), (axial_hbm, axial), (shear_hbm, shear))
        )
    ]
    for copy in chunks + body_copies + fields:
        copy.start()

    barrier = pltpu.get_barrier_semaphore()

    def greet(peer, carry):
        pl.semaphore_signal(barrier, inc=1, device_id=(other, peer), device_id_type=MESH)
        return carry

    lax.fori_loop(0, PEERS, greet, 0, unroll=8)
    column = [lax.rem(depth + i, DEPTH) * FLAT + flat for i in range(1, DEPTH)]
    near = [after, before] + column
    for peer in near:
        pl.semaphore_signal(barrier, inc=1, device_id=(region, peer), device_id_type=MESH)

    for copy in small:
        copy.wait()
    square = (ROWS, PEERS)
    sublane = lax.broadcasted_iota(jnp.int32, square, 0)
    lane = lax.broadcasted_iota(jnp.int32, square, 1)
    by_lane = jnp.broadcast_to(owner[...], square)
    by_sublane = by_lane.T
    same = by_lane == by_sublane
    rank = jnp.sum(jnp.where(same & (lane < sublane), 1, 0), axis=1, keepdims=True)
    target_column = jnp.broadcast_to(target[...], square).T
    index_vmem[...] = jnp.zeros(index_vmem.shape, jnp.int32)
    for r in range(SLOTS):
        chosen = (by_sublane == lane) & (rank == r)
        index = ROWS + jnp.sum(jnp.where(chosen, sublane - ROWS, 0), axis=0, keepdims=True)
        index_vmem[r : r + 1, :] = index
        row = jnp.sum(jnp.where(chosen, target_column, 0), axis=0, keepdims=True)
        rows_out[r, pl.ds(depth, 1), :] = row
    to_scalar = pltpu.make_async_copy(index_vmem, index_smem, small_sem.at[6])
    to_scalar.start()

    contrib[ROWS] = jnp.zeros((8, FACES), F32)
    for copy in faces:
        copy.wait()

    def weigh(z, carry):
        source = face[pl.ds(z, MOMENTS, stride=ROWS), :]
        source = jnp.concatenate([source, jnp.zeros((2, FACES), F32)], axis=0)
        source_high = source.astype(BF16).astype(F32)
        both = jnp.concatenate([source_high, source - source_high], axis=0).astype(BF16)
        matrix = weight[pl.ds(pl.multiple_of(z * FACES, FACES), FACES), :]
        high = matrix.astype(BF16)
        low = (matrix - high.astype(F32)).astype(BF16)
        product = lax.dot_general(
            both,
            jnp.concatenate([high, low], axis=0),
            (((1,), (1,)), ((), ())),
            preferred_element_type=F32,
        )
        contrib[z] = (
            product[:8, :FACES] + (product[8:, :FACES] + product[:8, FACES:])
        )
        return carry

    for c in range(CHUNKS):
        chunks[c].wait()
        lax.fori_loop(c * per_chunk, (c + 1) * per_chunk, weigh, 0, unroll=per_chunk)
    to_scalar.wait()

    pl.semaphore_wait(barrier, PEERS + len(near))

    for peer in column:
        row = rows_out.at[:, pl.ds(depth, 1)]
        pltpu.make_async_remote_copy(
            src_ref=row,
            dst_ref=row,
            send_sem=hop_send_sem,
            recv_sem=hop_recv_sem,
            device_id=(region, peer),
            device_id_type=MESH,
        ).start()

    def dispatch(peer, carry):
        for r in range(SLOTS):
            block = index_smem[r, peer]
            values = contrib[block]
            outgoing[pl.ds(MESSAGE * peer + MOMENTS * r, MOMENTS), :] = values[:MOMENTS]
        pltpu.make_async_remote_copy(
            src_ref=outgoing.at[pl.ds(MESSAGE * peer, MESSAGE)],
            dst_ref=incoming.at[pl.ds(MESSAGE * place, MESSAGE)],
            send_sem=send_sem,
            recv_sem=recv_sem,
            device_id=(other, peer),
            device_id_type=MESH,
        ).start()
        return carry


    for copy in body_copies:
        copy.wait()
    lanes = lax.broadcasted_iota(jnp.int32, (8, FACES), 1)

    def pack(i, carry):
        packed = jnp.zeros((8, FACES), F32)
        for k in range(MOMENTS):
            for layer in range(LAYERS):
                p = k * LAYERS + layer
                values = cells[pl.ds(pl.multiple_of(plane(k, layer + 1) + i * 8, 8), 8), :]
                packed = jnp.where(lanes == p, pltpu.roll(values, p + 1, 1), packed)
        rim_columns[pl.ds(pl.multiple_of(i * 8, 8), 8), :] = packed
        return carry

    lax.fori_loop(0, ROWS // 8, pack, 0, unroll=4)
    rim_out[...] = rim_columns[...].T[:PLANES]
    rim = pltpu.make_async_remote_copy(
        src_ref=rim_out,
        dst_ref=rim_in,
        send_sem=rim_send_sem,
        recv_sem=rim_recv_sem,
        device_id=(region, after),
        device_id_type=MESH,
    )
    rim.start()

    lax.fori_loop(0, PEERS, dispatch, 0, unroll=2)

    hop = pltpu.make_async_remote_copy(
        src_ref=rows_out.at[:, pl.ds(0, DEPTH - 1)],
        dst_ref=rows_out.at[:, pl.ds(0, DEPTH - 1)],
        send_sem=hop_send_sem,
        recv_sem=hop_recv_sem,
        device_id=(region, after),
        device_id_type=MESH,
    )
    hop.wait_recv()

    def spread(i, carry):
        pltpu.make_async_remote_copy(
            src_ref=rows_out,
            dst_ref=rows_in.at[:, pl.ds(pl.multiple_of(flat * DEPTH, DEPTH), DEPTH)],
            send_sem=rows_send_sem,
            recv_sem=rows_recv_sem,
            device_id=(other, depth * FLAT + i),
            device_id_type=MESH,
        ).start()
        return carry

    lax.fori_loop(0, FLAT, spread, 0)

    for k in range(MOMENTS):
        for edge in (0, LAYERS + 1):
            cells[pl.ds(plane(k, edge), ROWS), :] = jnp.zeros((ROWS, FACES), F32)

    for copy in fields:
        copy.wait()
    rim.wait_recv()
    unused = jnp.zeros((FACES - PLANES, ROWS), F32)
    rim_columns[...] = jnp.concatenate([rim_in[...], unused], axis=0).T
    lanes_block = lax.broadcasted_iota(jnp.int32, (BLOCK, FACES), 1)
    rows_block = lax.broadcasted_iota(jnp.int32, (BLOCK, FACES), 0)

    def advect(layer, i, at_interface):
        start = pl.multiple_of(i * BLOCK, BLOCK)
        at = pl.multiple_of(layer * ROWS + start, BLOCK)
        ca = azimuth[pl.ds(at, BLOCK), :]
        cr = radial[pl.ds(at, BLOCK), :]
        cz = axial[pl.ds(at, BLOCK), :]
        outward = cr > 0.0
        upward = cz > 0.0
        cr = jnp.abs(cr)
        cz = jnp.abs(cz)
        keep = 1.0 - ca - cr - cz
        at_edge = rows_block + start == jnp.where(upward, 0, ROWS - 1)
        cz = jnp.where(at_edge, 0.0, cz)
        rims = rim_columns[pl.ds(start, BLOCK), :]
        if at_interface:
            from_ghost = outward == (region == 1)
            ghost_weight[pl.ds(start, BLOCK), :] = jnp.where(from_ghost, cr, 0.0)
            cr = jnp.where(from_ghost, 0.0, cr)
        advected = []
        for k in range(MOMENTS):
            row = plane(k, layer + 1) + start
            m = cells[pl.ds(row, BLOCK), :]
            shift = lax.rem(2 * FACES - (k * LAYERS + layer), FACES)
            previous = jnp.where(
                lanes_block == 0, pltpu.roll(rims, shift, 1), pltpu.roll(m, 1, 1)
            )
            axial_below = cells[pl.ds(row - 1, BLOCK), :]
            axial_beyond = cells[pl.ds(row + 1, BLOCK), :]
            if at_interface:
                radial_side = cells[pl.ds(row + (2 * region - 1) * ROWS, BLOCK), :]
            else:
                below = cells[pl.ds(row - ROWS, BLOCK), :]
                beyond = cells[pl.ds(row + ROWS, BLOCK), :]
                radial_side = jnp.where(outward, below, beyond)
            advected.append(
                keep * m
                + ca * previous
                + cr * radial_side
                + cz * jnp.where(upward, axial_below, axial_beyond)
            )
        return advected

    def finish(layer, i, advected):
        start = pl.multiple_of(i * BLOCK, BLOCK)
        at = pl.multiple_of(layer * ROWS + start, BLOCK)
        result = sources(advected, shear[pl.ds(at, BLOCK), :])
        for k in range(MOMENTS):
            out_ref[k, layer, pl.ds(start, BLOCK), :] = result[k]

    def inner(n, carry):
        layer = region + n // (ROWS // BLOCK)
        i = lax.rem(n, ROWS // BLOCK)
        finish(layer, i, advect(layer, i, False))
        return carry

    lax.fori_loop(0, (LAYERS - 1) * (ROWS // BLOCK), inner, 0)

    def prepare(i, carry):
        advected = advect(interface, i, True)
        for k in range(MOMENTS):
            partial[pl.ds(pl.multiple_of(k * ROWS + i * BLOCK, BLOCK), BLOCK), :] = advected[k]
        return carry

    lax.fori_loop(0, ROWS // BLOCK, prepare, 0)

    rows = pltpu.make_async_remote_copy(
        src_ref=rows_in,
        dst_ref=rows_in,
        send_sem=rows_send_sem,
        recv_sem=rows_recv_sem,
        device_id=(other, me),
        device_id_type=MESH,
    )
    rows.wait_recv()
    mine = []
    for r in range(SLOTS):
        named = jnp.where(lane == me, rows_in[r], 0)
        named = jnp.sum(named, axis=1, keepdims=True)
        mine.append(jnp.where(named == lane, 1.0, 0.0).T)
    hits = jnp.concatenate(mine, axis=1).astype(BF16)

    whole = pltpu.make_async_remote_copy(
        src_ref=outgoing,
        dst_ref=incoming,
        send_sem=send_sem,
        recv_sem=recv_sem,
        device_id=(other, me),
        device_id_type=MESH,
    )
    whole.wait_recv()

    for k in range(MOMENTS):
        received = jnp.concatenate(
            [
                incoming[pl.ds(r * MOMENTS + k, PEERS, stride=MESSAGE), :]
                for r in range(SLOTS)
            ],
            axis=0,
        )
        high = received.astype(BF16)
        low = (received - high.astype(F32)).astype(BF16)
        summed = jnp.dot(
            hits, jnp.concatenate([high, low], axis=1), preferred_element_type=F32
        )
        ghost = summed[:, :FACES] + summed[:, FACES:]
        at = pl.ds(k * ROWS, ROWS)
        partial[at, :] = partial[at, :] + ghost_weight[...] * ghost

    def outer(i, carry):
        advected = [
            partial[pl.ds(pl.multiple_of(k * ROWS + i * BLOCK, BLOCK), BLOCK), :]
            for k in range(MOMENTS)
        ]
        finish(interface, i, advected)
        return carry

    lax.fori_loop(0, ROWS // BLOCK, outer, 0)
    whole.wait_send()
    rim.wait_send()
    hop.wait_send()
    rows.wait_send()


def on_device(
    moments, courant_azimuth, courant_radial, courant_axial, shear, owner, target, ami_weight
):
    shape = (MOMENTS, LAYERS, ROWS, FACES)
    field = (LAYERS * ROWS, FACES)
    dma = pltpu.SemaphoreType.DMA
    updated = pl.pallas_call(
        kernel,
        out_shape=jax.ShapeDtypeStruct(shape, F32),
        in_specs=[pl.BlockSpec(memory_space=pltpu.HBM)] * 8,
        out_specs=pl.BlockSpec(memory_space=pltpu.VMEM),
        scratch_shapes=[
            pltpu.VMEM((MOMENTS * (LAYERS + 2) * ROWS, FACES), F32),
            pltpu.VMEM(field, F32),
            pltpu.VMEM(field, F32),
            pltpu.VMEM(field, F32),
            pltpu.VMEM(field, F32),
            pltpu.VMEM((1, ROWS), jnp.int32),
            pltpu.VMEM((1, ROWS), jnp.int32),
            pltpu.VMEM((ROWS * FACES, FACES), F32),
            pltpu.VMEM((MOMENTS * ROWS, FACES), F32),
            pltpu.VMEM((ROWS + 1, 8, FACES), F32),
            pltpu.VMEM((8, PEERS), jnp.int32),
            pltpu.SMEM((8, PEERS), jnp.int32),
            pltpu.VMEM((MESSAGE * PEERS, FACES), F32),
            pltpu.VMEM((MESSAGE * PEERS, FACES), F32),
            pltpu.VMEM((ROWS, FACES), F32),
            pltpu.VMEM((PLANES, ROWS), F32),
            pltpu.VMEM((PLANES, ROWS), F32),
            pltpu.VMEM((SLOTS, DEPTH, PEERS), jnp.int32),
            pltpu.VMEM((SLOTS, PEERS, PEERS), jnp.int32),
            pltpu.VMEM((MOMENTS * ROWS, FACES), F32),
            pltpu.VMEM((ROWS, FACES), F32),
            dma((7,)),
            dma((2 * MOMENTS,)),
            dma((CHUNKS,)),
            dma,
            dma,
            dma,
            dma,
            dma,
            dma,
            dma,
            dma,
        ],
        compiler_params=pltpu.CompilerParams(
            collective_id=0, has_side_effects=True, vmem_limit_bytes=48 * 1024 * 1024
        ),
        name="transport",
    )(
        *[
            pltpu.with_memory_space_constraint(operand, pltpu.HBM)
            for operand in (
                moments.reshape(MOMENTS, LAYERS * ROWS, FACES),
                courant_azimuth.reshape(field),
                courant_radial.reshape(field),
                courant_axial.reshape(field),
                shear.reshape(field),
                owner.reshape(1, ROWS),
                target.reshape(1, ROWS),
                ami_weight.reshape(ROWS * FACES, FACES),
            )
        ]
    )
    return updated[None]


def solution(mesh):
    placed = (
        P("region", None, None, None, "cells"),
        P("region", None, None, "cells"),
        P("region", None, None, "cells"),
        P("region", None, None, "cells"),
        P("region", None, None, "cells"),
        P("region", "cells", None),
        P("region", "cells"),
        P("region", "cells", None, None),
    )
    return jax.shard_map(
        on_device,
        mesh=mesh,
        in_specs=placed,
        out_specs=P("region", None, None, None, "cells"),
        check_vma=False,
    )
```

```python
import functools

import jax
import jax.numpy as jnp
from jax import lax
from jax.experimental import pallas as pl
from jax.experimental.pallas import tpu as pltpu
from jax.sharding import PartitionSpec as P

MESH = pl.DeviceIdType.MESH
F32 = jnp.float32
BF16 = jnp.bfloat16
KAGG = 0.005
KBRK = 0.02
LAYERS = 4
ROWS = 128
FACES = 128
MOMENTS = 6
PEERS = 128
SLOTS = 2
PLANES = MOMENTS * LAYERS
MESSAGE = SLOTS * MOMENTS
DEPTH = 8
FLAT = PEERS // DEPTH
CHUNKS = 4
EARLY = 32
BLOCK = 32
CUBE_ROOT_2 = 2.0 ** (1.0 / 3.0)

THIRD_ANGLE = (
    0.5000000032577528,
    0.5773497198231888,
    -0.11109568329657703,
    0.053288656003267744,
    -0.03196129546407778,
    0.019675718215576045,
    -0.01032549308338918,
    0.003707686483927317,
    -0.0006393143691536856,
)


def third_angle(s):
    value = THIRD_ANGLE[-1] * s + THIRD_ANGLE[-2]
    for coefficient in THIRD_ANGLE[-3::-1]:
        value = value * s + coefficient
    return value


def quadrature(moment):
    mass = moment[0]
    inverse = 1.0 / mass
    n1, n2, n3, n4, n5 = [moment[degree] * inverse for degree in range(1, 6)]
    a0 = n1
    p1 = n2 - a0 * n1
    p2 = n3 - a0 * n2
    p3 = n4 - a0 * n3
    p4 = n5 - a0 * n4
    over_p1 = 1.0 / p1
    ratio = p2 * over_p1
    a1 = ratio - a0
    q2 = p3 - a1 * p2 - p1 * n2
    q3 = p4 - a1 * p3 - p1 * n3
    over_q2 = 1.0 / q2
    a2 = q3 * over_q2 - ratio
    b2 = q2 * over_p1
    centre = (a0 + a1 + a2) * (1.0 / 3.0)
    d0 = a0 - centre
    d1 = a1 - centre
    d2 = a2 - centre
    square = (d0 * d0 + d1 * d1 + d2 * d2 + 2.0 * (p1 + b2)) * (1.0 / 6.0)
    over_h = lax.rsqrt(square)
    h2 = 2.0 * square * over_h
    determ = d0 * (d1 * d2 - b2) - p1 * d2
    half_cosine = jnp.clip(0.25 * determ * (over_h * over_h * over_h), -0.5, 0.5)
    high = centre + h2 * third_angle(jnp.sqrt(0.5 + half_cosine))
    low = centre - h2 * third_angle(jnp.sqrt(0.5 - half_cosine))
    middle = 3.0 * centre - high - low
    nodes = [low, middle, high]
    weights = []
    for node in nodes:
        lead = node - a0
        trail = (node - a1) * lead - p1
        weights.append(mass / (1.0 + lead * lead * over_p1 + trail * trail * over_q2))
    return nodes, weights


def sources(moment, shear):
    nodes, weights = quadrature(moment)
    cubes = [node * node * node for node in nodes]
    merge = KAGG * shear
    split = KBRK * shear
    carried = [w * c for w, c in zip(weights, cubes)]
    born = [4.0 * w * a * merge for w, a in zip(weights, carried)]
    broken = [split * a for a in carried]
    lost = [2.0 * b + f for b, f in zip(born, broken)]
    terms, steps = [], []
    for first, second in ((0, 1), (0, 2), (1, 2)):
        summed = nodes[first] + nodes[second]
        pair = merge * (weights[first] * weights[second]) * (summed * summed * summed)
        lost[first] = lost[first] + pair
        lost[second] = lost[second] + pair
        terms.append(pair)
        steps.append(jnp.exp(jnp.log(cubes[first] + cubes[second]) * (1.0 / 3.0)))
    for index in range(3):
        terms += [born[index], 2.0 * broken[index], -lost[index]]
        node = nodes[index]
        steps += [CUBE_ROOT_2 * node, (1.0 / CUBE_ROOT_2) * node, node]
    result = []
    for degree in range(MOMENTS):
        if degree:
            terms = [term * step for term, step in zip(terms, steps)]
        total = moment[degree]
        for term in terms:
            total = total + term
        result.append(total)
    return result


def kernel(
    moments_hbm,
    azimuth_hbm,
    radial_hbm,
    axial_hbm,
    shear_hbm,
    owner_hbm,
    target_hbm,
    weight_hbm,
    out_ref,
    cells,
    azimuth,
    radial,
    axial,
    shear,
    owner,
    target,
    weight,
    face,
    contrib,
    index_vmem,
    index_smem,
    outgoing,
    incoming,
    rim_columns,
    rim_out,
    rim_in,
    rows_out,
    rows_in,
    partial,
    ghost_weight,
    small_sem,
    cell_sem,
    weight_sem,
    send_sem,
    recv_sem,
    rim_send_sem,
    rim_recv_sem,
    hop_send_sem,
    hop_recv_sem,
    rows_send_sem,
    rows_recv_sem,
):
    region = lax.axis_index("region")
    me = lax.axis_index("cells")
    other = 1 - region
    after = lax.rem(me + 1, PEERS)
    before = lax.rem(me + PEERS - 1, PEERS)
    interface = (LAYERS - 1) * other
    depth, flat = me // FLAT, lax.rem(me, FLAT)
    place = flat * DEPTH + depth
    per_chunk = ROWS // CHUNKS

    def plane(k, layer):
        return (k * (LAYERS + 2) + layer) * ROWS

    small = [
        pltpu.make_async_copy(owner_hbm, owner, small_sem.at[0]),
        pltpu.make_async_copy(target_hbm, target, small_sem.at[1]),
    ]
    for copy in small:
        copy.start()
    faces = [
        pltpu.make_async_copy(
            moments_hbm.at[k, pl.ds(pl.multiple_of(interface * ROWS, ROWS), ROWS)], face.at[pl.ds(k * ROWS, ROWS)], cell_sem.at[k]
        )
        for k in range(MOMENTS)
    ]
    for copy in faces:
        copy.start()
    chunks = [
        pltpu.make_async_copy(
            weight_hbm.at[pl.ds(c * per_chunk * FACES, per_chunk * FACES)],
            weight.at[pl.ds(c * per_chunk * FACES, per_chunk * FACES)],
            weight_sem.at[c],
        )
        for c in range(CHUNKS)
    ]
    body_copies = []
    for k in range(MOMENTS):
        body_copies.append(
            pltpu.make_async_copy(
                moments_hbm.at[k],
                cells.at[pl.ds(plane(k, 1), LAYERS * ROWS)],
                cell_sem.at[MOMENTS + k],
            )
        )
    fields = [
        pltpu.make_async_copy(source, destination, small_sem.at[2 + i])
        for i, (source, destination) in enumerate(
            ((azimuth_hbm, azimuth), (radial_hbm, radial), (axial_hbm, axial), (shear_hbm, shear))
        )
    ]
    for copy in chunks[:-1] + body_copies + chunks[-1:] + fields:
        copy.start()

    barrier = pltpu.get_barrier_semaphore()

    def greet(peer, carry):
        pl.semaphore_signal(barrier, inc=1, device_id=(other, peer), device_id_type=MESH)
        return carry

    lax.fori_loop(0, PEERS, greet, 0, unroll=8)
    column = [lax.rem(depth + i, DEPTH) * FLAT + flat for i in range(1, DEPTH)]
    near = [after, before] + column
    for peer in near:
        pl.semaphore_signal(barrier, inc=1, device_id=(region, peer), device_id_type=MESH)

    for copy in small:
        copy.wait()
    square = (ROWS, PEERS)
    sublane = lax.broadcasted_iota(jnp.int32, square, 0)
    lane = lax.broadcasted_iota(jnp.int32, square, 1)
    by_lane = jnp.broadcast_to(owner[...], square)
    by_sublane = by_lane.T
    same = by_lane == by_sublane
    rank = jnp.sum(jnp.where(same & (lane < sublane), 1, 0), axis=1, keepdims=True)
    target_column = jnp.broadcast_to(target[...], square).T
    index_vmem[...] = jnp.zeros(index_vmem.shape, jnp.int32)
    for r in range(SLOTS):
        chosen = (by_sublane == lane) & (rank == r)
        index = ROWS + jnp.sum(jnp.where(chosen, sublane - ROWS, 0), axis=0, keepdims=True)
        index_vmem[r : r + 1, :] = index
        row = jnp.sum(jnp.where(chosen, target_column, 0), axis=0, keepdims=True)
        rows_out[r, pl.ds(depth, 1), :] = row
    to_scalar = pltpu.make_async_copy(index_vmem, index_smem, small_sem.at[6])
    to_scalar.start()

    contrib[ROWS] = jnp.zeros((8, FACES), F32)
    for copy in faces:
        copy.wait()

    def weigh(z, carry):
        source = face[pl.ds(z, MOMENTS, stride=ROWS), :]
        source = jnp.concatenate([source, jnp.zeros((2, FACES), F32)], axis=0)
        source_high = source.astype(BF16).astype(F32)
        both = jnp.concatenate([source_high, source - source_high], axis=0).astype(BF16)
        matrix = weight[pl.ds(pl.multiple_of(z * FACES, FACES), FACES), :]
        high = matrix.astype(BF16)
        low = (matrix - high.astype(F32)).astype(BF16)
        product = lax.dot_general(
            both,
            jnp.concatenate([high, low], axis=0),
            (((1,), (1,)), ((), ())),
            preferred_element_type=F32,
        )
        contrib[z] = (
            product[:8, :FACES] + (product[8:, :FACES] + product[:8, FACES:])
        )
        return carry

    for c in range(CHUNKS - 1):
        chunks[c].wait()
        lax.fori_loop(c * per_chunk, (c + 1) * per_chunk, weigh, 0, unroll=per_chunk)

    for copy in body_copies:
        copy.wait()
    lanes = lax.broadcasted_iota(jnp.int32, (8, FACES), 1)

    def pack(i, carry):
        packed = jnp.zeros((8, FACES), F32)
        for k in range(MOMENTS):
            for layer in range(LAYERS):
                p = k * LAYERS + layer
                values = cells[pl.ds(pl.multiple_of(plane(k, layer + 1) + i * 8, 8), 8), :]
                packed = jnp.where(lanes == p, pltpu.roll(values, p + 1, 1), packed)
        rim_columns[pl.ds(pl.multiple_of(i * 8, 8), 8), :] = packed
        return carry

    lax.fori_loop(0, ROWS // 8, pack, 0, unroll=4)
    rim_out[...] = rim_columns[...].T[:PLANES]
    for c in range(CHUNKS - 1, CHUNKS):
        chunks[c].wait()
        lax.fori_loop(c * per_chunk, (c + 1) * per_chunk, weigh, 0, unroll=per_chunk)
    to_scalar.wait()

    pl.semaphore_wait(barrier, PEERS + len(near))

    for peer in column:
        row = rows_out.at[:, pl.ds(depth, 1)]
        pltpu.make_async_remote_copy(
            src_ref=row,
            dst_ref=row,
            send_sem=hop_send_sem,
            recv_sem=hop_recv_sem,
            device_id=(region, peer),
            device_id_type=MESH,
        ).start()

    def dispatch(peer, carry):
        for r in range(SLOTS):
            block = index_smem[r, peer]
            values = contrib[block]
            outgoing[pl.ds(MESSAGE * peer + MOMENTS * r, MOMENTS), :] = values[:MOMENTS]
        pltpu.make_async_remote_copy(
            src_ref=outgoing.at[pl.ds(MESSAGE * peer, MESSAGE)],
            dst_ref=incoming.at[pl.ds(MESSAGE * place, MESSAGE)],
            send_sem=send_sem,
            recv_sem=recv_sem,
            device_id=(other, peer),
            device_id_type=MESH,
        ).start()
        return carry


    rim = pltpu.make_async_remote_copy(
        src_ref=rim_out,
        dst_ref=rim_in,
        send_sem=rim_send_sem,
        recv_sem=rim_recv_sem,
        device_id=(region, after),
        device_id_type=MESH,
    )
    rim.start()

    lax.fori_loop(0, PEERS, dispatch, 0, unroll=2)

    hop = pltpu.make_async_remote_copy(
        src_ref=rows_out.at[:, pl.ds(0, DEPTH - 1)],
        dst_ref=rows_out.at[:, pl.ds(0, DEPTH - 1)],
        send_sem=hop_send_sem,
        recv_sem=hop_recv_sem,
        device_id=(region, after),
        device_id_type=MESH,
    )
    hop.wait_recv()

    def spread(i, carry):
        pltpu.make_async_remote_copy(
            src_ref=rows_out,
            dst_ref=rows_in.at[:, pl.ds(pl.multiple_of(flat * DEPTH, DEPTH), DEPTH)],
            send_sem=rows_send_sem,
            recv_sem=rows_recv_sem,
            device_id=(other, depth * FLAT + i),
            device_id_type=MESH,
        ).start()
        return carry

    lax.fori_loop(0, FLAT, spread, 0)

    for k in range(MOMENTS):
        for edge in (0, LAYERS + 1):
            cells[pl.ds(plane(k, edge), ROWS), :] = jnp.zeros((ROWS, FACES), F32)

    for copy in fields:
        copy.wait()
    rim.wait_recv()
    unused = jnp.zeros((FACES - PLANES, ROWS), F32)
    rim_columns[...] = jnp.concatenate([rim_in[...], unused], axis=0).T
    lanes_block = lax.broadcasted_iota(jnp.int32, (BLOCK, FACES), 1)
    rows_block = lax.broadcasted_iota(jnp.int32, (BLOCK, FACES), 0)

    def advect(layer, i, at_interface):
        start = pl.multiple_of(i * BLOCK, BLOCK)
        at = pl.multiple_of(layer * ROWS + start, BLOCK)
        ca = azimuth[pl.ds(at, BLOCK), :]
        cr = radial[pl.ds(at, BLOCK), :]
        cz = axial[pl.ds(at, BLOCK), :]
        outward = cr > 0.0
        upward = cz > 0.0
        cr = jnp.abs(cr)
        cz = jnp.abs(cz)
        keep = 1.0 - ca - cr - cz
        at_edge = rows_block + start == jnp.where(upward, 0, ROWS - 1)
        cz = jnp.where(at_edge, 0.0, cz)
        rims = rim_columns[pl.ds(start, BLOCK), :]
        if at_interface:
            from_ghost = outward == (region == 1)
            ghost_weight[pl.ds(start, BLOCK), :] = jnp.where(from_ghost, cr, 0.0)
            cr = jnp.where(from_ghost, 0.0, cr)
        advected = []
        for k in range(MOMENTS):
            row = plane(k, layer + 1) + start
            m = cells[pl.ds(row, BLOCK), :]
            shift = lax.rem(2 * FACES - (k * LAYERS + layer), FACES)
            previous = jnp.where(
                lanes_block == 0, pltpu.roll(rims, shift, 1), pltpu.roll(m, 1, 1)
            )
            axial_below = cells[pl.ds(row - 1, BLOCK), :]
            axial_beyond = cells[pl.ds(row + 1, BLOCK), :]
            if at_interface:
                radial_side = cells[pl.ds(row + (2 * region - 1) * ROWS, BLOCK), :]
            else:
                below = cells[pl.ds(row - ROWS, BLOCK), :]
                beyond = cells[pl.ds(row + ROWS, BLOCK), :]
                radial_side = jnp.where(outward, below, beyond)
            advected.append(
                keep * m
                + ca * previous
                + cr * radial_side
                + cz * jnp.where(upward, axial_below, axial_beyond)
            )
        return advected

    def finish(layer, i, advected):
        start = pl.multiple_of(i * BLOCK, BLOCK)
        at = pl.multiple_of(layer * ROWS + start, BLOCK)
        result = sources(advected, shear[pl.ds(at, BLOCK), :])
        for k in range(MOMENTS):
            out_ref[k, layer, pl.ds(start, BLOCK), :] = result[k]

    def inner(n, carry):
        layer = region + n // (ROWS // BLOCK)
        i = lax.rem(n, ROWS // BLOCK)
        finish(layer, i, advect(layer, i, False))
        return carry

    lax.fori_loop(0, (LAYERS - 1) * (ROWS // BLOCK), inner, 0)

    def prepare(i, carry):
        advected = advect(interface, i, True)
        for k in range(MOMENTS):
            partial[pl.ds(pl.multiple_of(k * ROWS + i * BLOCK, BLOCK), BLOCK), :] = advected[k]
        return carry

    lax.fori_loop(0, ROWS // BLOCK, prepare, 0)

    rows = pltpu.make_async_remote_copy(
        src_ref=rows_in,
        dst_ref=rows_in,
        send_sem=rows_send_sem,
        recv_sem=rows_recv_sem,
        device_id=(other, me),
        device_id_type=MESH,
    )
    rows.wait_recv()
    mine = []
    for r in range(SLOTS):
        named = jnp.where(lane == me, rows_in[r], 0)
        named = jnp.sum(named, axis=1, keepdims=True)
        mine.append(jnp.where(named == lane, 1.0, 0.0).T)
    hits = jnp.concatenate(mine, axis=1).astype(BF16)

    whole = pltpu.make_async_remote_copy(
        src_ref=outgoing,
        dst_ref=incoming,
        send_sem=send_sem,
        recv_sem=recv_sem,
        device_id=(other, me),
        device_id_type=MESH,
    )
    whole.wait_recv()

    for k in range(MOMENTS):
        received = jnp.concatenate(
            [
                incoming[pl.ds(r * MOMENTS + k, PEERS, stride=MESSAGE), :]
                for r in range(SLOTS)
            ],
            axis=0,
        )
        high = received.astype(BF16)
        low = (received - high.astype(F32)).astype(BF16)
        summed = jnp.dot(
            hits, jnp.concatenate([high, low], axis=1), preferred_element_type=F32
        )
        ghost = summed[:, :FACES] + summed[:, FACES:]
        at = pl.ds(k * ROWS, ROWS)
        partial[at, :] = partial[at, :] + ghost_weight[...] * ghost

    def outer(i, carry):
        advected = [
            partial[pl.ds(pl.multiple_of(k * ROWS + i * BLOCK, BLOCK), BLOCK), :]
            for k in range(MOMENTS)
        ]
        finish(interface, i, advected)
        return carry

    lax.fori_loop(0, ROWS // BLOCK, outer, 0)
    whole.wait_send()
    rim.wait_send()
    hop.wait_send()
    rows.wait_send()


def on_device(
    moments, courant_azimuth, courant_radial, courant_axial, shear, owner, target, ami_weight
):
    shape = (MOMENTS, LAYERS, ROWS, FACES)
    field = (LAYERS * ROWS, FACES)
    dma = pltpu.SemaphoreType.DMA
    updated = pl.pallas_call(
        kernel,
        out_shape=jax.ShapeDtypeStruct(shape, F32),
        in_specs=[pl.BlockSpec(memory_space=pltpu.HBM)] * 8,
        out_specs=pl.BlockSpec(memory_space=pltpu.VMEM),
        scratch_shapes=[
            pltpu.VMEM((MOMENTS * (LAYERS + 2) * ROWS, FACES), F32),
            pltpu.VMEM(field, F32),
            pltpu.VMEM(field, F32),
            pltpu.VMEM(field, F32),
            pltpu.VMEM(field, F32),
            pltpu.VMEM((1, ROWS), jnp.int32),
            pltpu.VMEM((1, ROWS), jnp.int32),
            pltpu.VMEM((ROWS * FACES, FACES), F32),
            pltpu.VMEM((MOMENTS * ROWS, FACES), F32),
            pltpu.VMEM((ROWS + 1, 8, FACES), F32),
            pltpu.VMEM((8, PEERS), jnp.int32),
            pltpu.SMEM((8, PEERS), jnp.int32),
            pltpu.VMEM((MESSAGE * PEERS, FACES), F32),
            pltpu.VMEM((MESSAGE * PEERS, FACES), F32),
            pltpu.VMEM((ROWS, FACES), F32),
            pltpu.VMEM((PLANES, ROWS), F32),
            pltpu.VMEM((PLANES, ROWS), F32),
            pltpu.VMEM((SLOTS, DEPTH, PEERS), jnp.int32),
            pltpu.VMEM((SLOTS, PEERS, PEERS), jnp.int32),
            pltpu.VMEM((MOMENTS * ROWS, FACES), F32),
            pltpu.VMEM((ROWS, FACES), F32),
            dma((7,)),
            dma((2 * MOMENTS,)),
            dma((CHUNKS,)),
            dma,
            dma,
            dma,
            dma,
            dma,
            dma,
            dma,
            dma,
        ],
        compiler_params=pltpu.CompilerParams(
            collective_id=0, has_side_effects=True, vmem_limit_bytes=48 * 1024 * 1024
        ),
        name="transport",
    )(
        *[
            pltpu.with_memory_space_constraint(operand, pltpu.HBM)
            for operand in (
                moments.reshape(MOMENTS, LAYERS * ROWS, FACES),
                courant_azimuth.reshape(field),
                courant_radial.reshape(field),
                courant_axial.reshape(field),
                shear.reshape(field),
                owner.reshape(1, ROWS),
                target.reshape(1, ROWS),
                ami_weight.reshape(ROWS * FACES, FACES),
            )
        ]
    )
    return updated[None]


def solution(mesh):
    placed = (
        P("region", None, None, None, "cells"),
        P("region", None, None, "cells"),
        P("region", None, None, "cells"),
        P("region", None, None, "cells"),
        P("region", None, None, "cells"),
        P("region", "cells", None),
        P("region", "cells"),
        P("region", "cells", None, None),
    )
    return jax.shard_map(
        on_device,
        mesh=mesh,
        in_specs=placed,
        out_specs=P("region", None, None, None, "cells"),
        check_vma=False,
    )
```
